32 devices in a mesh: face: 4 (over x, core), tile: 8 (over z, y).
Axes of the slice: x: 2, y: 2, z: 4, core: 2. Of those that a mesh axis runs over, the one named last changes fastest.
Arguments:
- field_in: bfloat16 [12, 48, 256, 256], P('face', None, 'tile'), may hold values from -6 to 6
- out_grad: bfloat16 [12, 48, 256, 256], P('face', None, 'tile'), may hold values from -6 to 6
- weight_first: bfloat16 [48, 48, 3, 3], replicated, may hold values from -0.3125 to 0.3125
- bias_first: float32 [48], replicated, may hold values from -3 to 3
- weight_second: bfloat16 [48, 48, 3, 3], replicated, may hold values from -0.3125 to 0.3125
- bias_second: float32 [48], replicated, may hold values from -3 to 3
- face_links: int32 [12, 4, 3], replicated, may hold values from 0 to 11, as said below
- corner_rules: int32 [12, 4], replicated, may hold values from 0 to 1
Outputs:
- output_field: bfloat16 [12, 48, 256, 256], P('face', None, 'tile')
- grad_field: bfloat16 [12, 48, 256, 256], P('face', None, 'tile')
- grad_weight_first: float32 [48, 48, 3, 3], replicated
- grad_bias_first: float32 [48], replicated
- grad_weight_second: float32 [48, 48, 3, 3], replicated
- grad_bias_second: float32 [48], replicated
The draws below stay inside these ranges and needn't reach their ends.
Inputs may be any that keep to these rules, and one draw needn't show every extreme that they name: face_links[f, e] = (g, e2, r) glues edge e of face f to edge e2 of face g; r = 1 when positions along the two edges run in opposite directions. The gluing is a pairing: (g, e2) differs from (f, e) and face_links[g, e2] = (f, e, r). The partner face lies in 0..11, the edge in 0..3, the flag in 0..1.
All inputs are finite; a program needn't handle non-finite values.
Results may differ from the reference program's by a relative error of at most 0.0055.
The reference program's roundings to bfloat16 on the way count: a program that leaves them out, or rounds other values in their place, can miss the bound.
Values may be sent and summed in bfloat16 or wider, within the bound.
A program may use at most 256 MiB of HBM per device.

```python
import jax
import jax.numpy as jnp
from jax import lax

C = 48
FACES = 12
NSIDE = 256


def draw_face_links(key, part):
    order = jax.random.permutation(key, 4 * FACES).astype(jnp.int32)
    flips = jax.random.randint(jax.random.fold_in(key, 7), (2 * FACES,), 0, 2).astype(jnp.int32)
    first_edge = order[0::2]
    second_edge = order[1::2]
    table = jnp.zeros((4 * FACES, 3), jnp.int32)
    table = table.at[first_edge].set(jnp.stack([second_edge // 4, second_edge % 4, flips], axis=1))
    table = table.at[second_edge].set(jnp.stack([first_edge // 4, first_edge % 4, flips], axis=1))
    return table.reshape(FACES, 4, 3)


def with_ends(result, rng, low, high):
    longest = result.shape.index(max(result.shape))
    spots = []
    for shift in (0, 1):
        where = [jax.random.randint(jax.random.fold_in(rng, axis), (), 0, length) for axis, length in enumerate(result.shape)]
        where[longest] = (where[longest] + shift) % result.shape[longest]
        spots.append(tuple(where))
    return result.at[spots[0]].set(low).at[spots[1]].set(high)


def block_levels(own_key, shape, split, smallest, largest):
    gain = 1.0
    for position, parts in split:
        heights = jax.random.uniform(jax.random.fold_in(jax.random.fold_in(own_key, 6), position), (parts,), jnp.float32, smallest / len(split), largest / len(split))
        gain = gain * jnp.repeat(jnp.exp(heights), shape[position] // parts).reshape((-1,) + (1,) * (len(shape) - 1 - position))
    return gain


def gaussian(key, extent, width, most, shards=(), held_as=jnp.bfloat16):
    result = width * jax.random.normal(key, extent, jnp.float32)
    if shards:
        result = result * block_levels(key, extent, shards, -0.22, 0.18)
    return jnp.clip(result, -most, most).astype(held_as)


def setup_inputs(seed: int = 0) -> dict:
    seeds = jax.random.split(jax.random.key(seed), 9)
    field_in = gaussian(seeds[0], (FACES, C, NSIDE, NSIDE), 1.0, 6.0, ((0, 4), (2, 8)))
    out_grad = gaussian(seeds[1], (FACES, C, NSIDE, NSIDE), 1.0, 6.0, ((0, 4), (2, 8)))
    weight_first = gaussian(seeds[2], (C, C, 3, 3), (9 * C) ** -0.5, 0.3125)
    bias_first = gaussian(seeds[3], (C,), 0.5, 3.0, (), jnp.float32)
    weight_second = gaussian(seeds[4], (C, C, 3, 3), (9 * C) ** -0.5, 0.3125)
    bias_second = gaussian(seeds[5], (C,), 0.5, 3.0, (), jnp.float32)
    face_links = draw_face_links(jax.random.fold_in(seeds[8], 71), 0)
    corner_rules = with_ends(jax.random.randint(seeds[7], (FACES, 4), 0, 2), jax.random.fold_in(seeds[7], 1), 0, 1).astype(jnp.int32)
    return {"field_in": field_in, "out_grad": out_grad, "weight_first": weight_first, "bias_first": bias_first, "weight_second": weight_second, "bias_second": bias_second, "face_links": face_links, "corner_rules": corner_rules}


INV_ROOT_TWO = 0.7071067811865476
INV_ROOT_TWO_PI = 0.3989422804014327

def gelu_pair(values):
    normal_cdf = 0.5 * (1.0 + lax.erf(values * INV_ROOT_TWO))
    normal_pdf = jnp.exp(-0.5 * values * values) * INV_ROOT_TWO_PI
    return (values * normal_cdf, normal_cdf + values * normal_pdf)

def convolve(padded, weight):
    return lax.conv_general_dilated(padded.astype(jnp.float32), weight.astype(jnp.float32), (1, 1), 'VALID', dimension_numbers=('NCHW', 'OIHW', 'NCHW'), precision=lax.Precision.HIGHEST)

def edge_lines(activation):
    return jnp.stack([activation[:, :, 0, :], activation[:, :, -1, :], activation[:, :, :, 0], activation[:, :, :, -1]], axis=1)

def partner(lines_all, face_links):
    source = lines_all[face_links[:, :, 0], face_links[:, :, 1]]
    flipped = source[..., ::-1]
    return jnp.where((face_links[:, :, 2] == 1)[:, :, None, None], flipped, source)

def fill_seams(activation, face_links, corner_rules):
    ghosts = partner(edge_lines(activation), face_links)
    north_line, south_line, west_line, east_line = (ghosts[:, 0], ghosts[:, 1], ghosts[:, 2], ghosts[:, 3])
    corner_code = (corner_rules == 0)[:, :, None]
    corner_nw = jnp.where(corner_code[:, 0], north_line[:, :, 0], west_line[:, :, 0])
    corner_ne = jnp.where(corner_code[:, 1], north_line[:, :, -1], east_line[:, :, 0])
    corner_sw = jnp.where(corner_code[:, 2], south_line[:, :, 0], west_line[:, :, -1])
    corner_se = jnp.where(corner_code[:, 3], south_line[:, :, -1], east_line[:, :, -1])
    middle = jnp.concatenate([west_line[:, :, :, None], activation, east_line[:, :, :, None]], axis=3)
    top_row = jnp.concatenate([corner_nw[:, :, None], north_line, corner_ne[:, :, None]], axis=2)
    bottom_row = jnp.concatenate([corner_sw[:, :, None], south_line, corner_se[:, :, None]], axis=2)
    return jnp.concatenate([top_row[:, :, None], middle, bottom_row[:, :, None]], axis=2)

def back_conv(cotangent, weight):
    padded = jnp.pad(cotangent, ((0, 0), (0, 0), (2, 2), (2, 2)))
    flipped = jnp.transpose(weight[:, :, ::-1, ::-1], (1, 0, 2, 3))
    return convolve(padded, flipped)

def unfold(pad_grad, face_links, corner_rules):
    north_line = pad_grad[:, :, 0, 1:-1]
    south_line = pad_grad[:, :, -1, 1:-1]
    west_line = pad_grad[:, :, 1:-1, 0]
    east_line = pad_grad[:, :, 1:-1, -1]
    corner_nw = pad_grad[:, :, 0, 0]
    corner_ne = pad_grad[:, :, 0, -1]
    corner_sw = pad_grad[:, :, -1, 0]
    corner_se = pad_grad[:, :, -1, -1]
    corner_code = corner_rules[:, :, None]
    zero = jnp.float32(0.0)
    north_line = north_line.at[:, :, 0].add(jnp.where(corner_code[:, 0] == 0, corner_nw, zero))
    north_line = north_line.at[:, :, -1].add(jnp.where(corner_code[:, 1] == 0, corner_ne, zero))
    south_line = south_line.at[:, :, 0].add(jnp.where(corner_code[:, 2] == 0, corner_sw, zero))
    south_line = south_line.at[:, :, -1].add(jnp.where(corner_code[:, 3] == 0, corner_se, zero))
    west_line = west_line.at[:, :, 0].add(jnp.where(corner_code[:, 0] == 1, corner_nw, zero))
    west_line = west_line.at[:, :, -1].add(jnp.where(corner_code[:, 2] == 1, corner_sw, zero))
    east_line = east_line.at[:, :, 0].add(jnp.where(corner_code[:, 1] == 1, corner_ne, zero))
    east_line = east_line.at[:, :, -1].add(jnp.where(corner_code[:, 3] == 1, corner_se, zero))
    lines_grad = jnp.stack([north_line, south_line, west_line, east_line], axis=1).astype(jnp.bfloat16)
    returned = partner(lines_grad, face_links).astype(jnp.float32)
    interior = pad_grad[:, :, 1:-1, 1:-1]
    interior = interior.at[:, :, 0, :].add(returned[:, 0])
    interior = interior.at[:, :, -1, :].add(returned[:, 1])
    interior = interior.at[:, :, :, 0].add(returned[:, 2])
    interior = interior.at[:, :, :, -1].add(returned[:, 3])
    return interior

def weight_grad(cotangent, padded):
    row_count, col_count = (cotangent.shape[2], cotangent.shape[3])
    channels = cotangent.shape[1]
    grad_wide = cotangent.astype(jnp.float32)
    products = []
    for row_off in range(3):
        for col_off in range(3):
            window = padded[:, :, row_off:row_off + row_count, col_off:col_off + col_count].astype(jnp.float32)
            products.append(jnp.einsum('ncrs,nirs->ci', grad_wide, window, precision=lax.Precision.HIGHEST))
    return jnp.stack(products).reshape(3, 3, channels, channels).transpose(2, 3, 0, 1)

def reference(field_in, out_grad, weight_first, bias_first, weight_second, bias_second, face_links, corner_rules):
    padded_first = fill_seams(field_in, face_links, corner_rules)
    pre_first = convolve(padded_first, weight_first) + bias_first[None, :, None, None]
    gelu_first, slope_first = gelu_pair(pre_first)
    hidden = gelu_first.astype(jnp.bfloat16)
    padded_second = fill_seams(hidden, face_links, corner_rules)
    pre_second = convolve(padded_second, weight_second) + bias_second[None, :, None, None]
    gelu_second, slope_second = gelu_pair(pre_second)
    output_field = gelu_second.astype(jnp.bfloat16)
    grad_second = (out_grad.astype(jnp.float32) * slope_second).astype(jnp.bfloat16)
    grad_weight_second = weight_grad(grad_second, padded_second) / NSIDE
    grad_bias_second = lax.optimization_barrier(jnp.sum(grad_second.astype(jnp.float32), axis=(0, 2, 3))) / NSIDE
    grad_hidden = unfold(back_conv(grad_second, weight_second), face_links, corner_rules)
    grad_first = (grad_hidden * slope_first).astype(jnp.bfloat16)
    grad_weight_first = weight_grad(grad_first, padded_first) / NSIDE
    grad_bias_first = lax.optimization_barrier(jnp.sum(grad_first.astype(jnp.float32), axis=(0, 2, 3))) / NSIDE
    grad_field = unfold(back_conv(grad_first, weight_first), face_links, corner_rules).astype(jnp.bfloat16)
    return (output_field, grad_field, grad_weight_first, grad_bias_first, grad_weight_second, grad_bias_second)
```

```python
import functools

import jax
import jax.numpy as jnp
from jax import lax
from jax.experimental import pallas as pl
from jax.experimental.pallas import tpu as pltpu
from jax.sharding import PartitionSpec as P

INV_ROOT_TWO = 0.7071067811865476
INV_ROOT_TWO_PI = 0.3989422804014327
F32 = jnp.float32
BF16 = jnp.bfloat16
LANES = 128
MESH_ID = pl.DeviceIdType.MESH
EDGES = 4
GROUP = 16


def gelu_pair(values):
    normal_cdf = 0.5 * (1.0 + lax.erf(values * INV_ROOT_TWO))
    normal_pdf = jnp.exp(-0.5 * values * values) * INV_ROOT_TWO_PI
    return (values * normal_cdf, normal_cdf + values * normal_pdf)


def one_hot(rows, target):
    row = lax.broadcasted_iota(jnp.int32, (rows, target.shape[1]), 0)
    return jnp.where(row == target, 1.0, 0.0).astype(BF16)


def turn(a, shift):
    return pltpu.roll(a, shift % LANES, 1)


def fused_kernel(
    faces_axis, tiles, links, rules, x_ref, og_ref, wst_ref, b_ref, u_ref,
    out_ref, gf_ref, gw_ref,
    xb, hb, g2b, g1b, ogb, rowsb, slope_ref, cp, packs0, packs1, packs2, packs3, gp, gpn, full, seg_out, seg_in, line_in, ns_out, spread,
    addcol, addrow, part, landed,
    s_halo, r_halo, s_direct, s_fwd, s_ns, r_packs, s_ends, r_ends, s_seg, r_seg, s_sum, r_sum, s_res, r_res,
):
    nf, C, rows, width = x_ref.shape
    packs = (packs0, packs1, packs2, packs3)
    slots = packs0.shape[1]
    n_dev = faces_axis * tiles
    face = lax.axis_index("face")
    tile = lax.axis_index("tile")
    me = face * tiles + tile
    last = tiles - 1
    mirror_tile = last - tile
    half = tiles // 2
    lane = lax.broadcasted_iota(jnp.int32, (C, LANES), 1)
    even = lane % 2 == 0
    is_top = tile == 0
    is_bottom = tile == last
    top_f = jnp.where(is_top, 1.0, 0.0)
    bottom_f = jnp.where(is_bottom, 1.0, 0.0)
    upper_half = jnp.where(tile >= half, 1, 0)
    peer = lax.rem(face + 2, faces_axis)
    sibling = face + 1 - 2 * lax.rem(face, 2)
    sibling_peer = lax.rem(sibling + 2, faces_axis)

    def at(j):
        return (lax.div(j, tiles), lax.rem(j, tiles))

    def each_other(body):
        def step(j, carry):
            @pl.when(j != me)
            def _():
                body(j)

            return carry

        lax.fori_loop(0, n_dev, step, 0)

    barrier = pltpu.get_barrier_semaphore()
    each_other(lambda j: pl.semaphore_signal(barrier, inc=1, device_id=at(j), device_id_type=MESH_ID))

    def to_rows(src, dst, first):
        for f in range(nf):
            for r0 in range(0, rows, GROUP):
                n = min(GROUP, rows - r0)
                for c0 in range(0, C, GROUP):
                    block = src[f, c0 : c0 + GROUP, r0 : r0 + n]
                    if n < GROUP:
                        block = jnp.swapaxes(block.astype(F32), 0, 1).astype(BF16)
                    else:
                        block = jnp.swapaxes(block, 0, 1)
                    dst[f, first + r0 : first + r0 + n, c0 : c0 + GROUP] = block

    def from_rows(src, dst):
        for f in range(nf):
            for r0 in range(0, rows, GROUP):
                n = min(GROUP, rows - r0)
                for c0 in range(0, C, GROUP):
                    block = src[f, r0 : r0 + n, c0 : c0 + GROUP]
                    if n < GROUP:
                        block = jnp.swapaxes(block.astype(F32), 0, 1).astype(BF16)
                    else:
                        block = jnp.swapaxes(block, 0, 1)
                    dst[f, c0 : c0 + GROUP, r0 : r0 + n] = block

    def keep(acc, r, lo, hi):
        mixed = turn(jnp.where(lane == LANES - 1, hi, lo), 2 * r)
        return jnp.where((lane == 2 * r) | (lane == (2 * r - 1) % LANES), mixed, acc)

    def copy(src, dst, send, recv, device):
        return pltpu.make_async_remote_copy(src, dst, send, recv, device, MESH_ID)

    ns_base = 2 * faces_axis

    def halo_copies(k, buf):
        up = copy(buf.at[:, 1], buf.at[:, rows + 1], s_halo.at[k, 0], r_halo.at[k, 1], (face, tile - 1))
        down = copy(buf.at[:, rows], buf.at[:, 0], s_halo.at[k, 1], r_halo.at[k, 0], (face, tile + 1))
        return up, down

    def direct_copies(k):
        own = packs[k].at[face]
        here = face
        there = faces_axis + face
        return [
            copy(own, packs[k].at[there], s_direct.at[k, 0], r_packs.at[k, there], (face, mirror_tile)),
            copy(own, packs[k].at[there], s_direct.at[k, 1], r_packs.at[k, there], (peer, mirror_tile)),
            copy(own, packs[k].at[here], s_direct.at[k, 2], r_packs.at[k, here], (peer, tile)),
            copy(own, packs[k].at[here], s_direct.at[k, 3], r_packs.at[k, here], (sibling, tile)),
        ]

    def ns_slot():
        return ns_base + jnp.where(is_top, 0, 1) * faces_axis + face

    def ns_copies(k, t):
        src = ns_out.at[k, min(t, last - t)]
        slot = ns_slot()
        return [
            copy(src, packs[k].at[slot], s_ns.at[k, t], r_packs.at[k, slot], (face, t)),
            copy(src, packs[k].at[slot], s_ns.at[k, tiles + t], r_packs.at[k, slot], (peer, t)),
        ]

    def forward_slots():
        return [faces_axis + face, peer, faces_axis + peer] + [
            ns_base + n * faces_axis + q for n in range(2) for q in (face, peer)
        ]

    def arriving_slots():
        return [sibling, faces_axis + sibling, sibling_peer, faces_axis + sibling_peer] + [
            ns_base + n * faces_axis + q for n in range(2) for q in (sibling, sibling_peer)
        ]

    def forward_copy(k, i, slot):
        ref = packs[k].at[slot]
        return copy(ref, ref, s_fwd.at[k, i], r_packs.at[k, slot], (sibling, tile))

    def ends_copies(k):
        return (
            copy(gp.at[k], gpn.at[k, 1], s_ends.at[k, 0], r_ends.at[k, 1], (face, tile - 1)),
            copy(gp.at[k], gpn.at[k, 0], s_ends.at[k, 1], r_ends.at[k, 0], (face, tile + 1)),
        )

    def seg_copies(k):
        dst = seg_in.at[k, tile]
        return (
            copy(seg_out.at[k, 0], dst, s_seg.at[k, 0], r_seg.at[k, tile], (face, 0)),
            copy(seg_out.at[k, 1], dst, s_seg.at[k, 1], r_seg.at[k, tile], (face, last)),
        )

    def start_exchange(k, buf):
        for slot in range(slots):
            faces_here = [f for f in range(nf) if f // 2 == slot]
            packed = turn(cp[faces_here[0]], 1)
            if len(faces_here) > 1:
                packed = jnp.where(lane < 64, packed, turn(cp[faces_here[1]], 65))
            packs[k][face, slot] = packed.astype(BF16)
        for c in direct_copies(k):
            c.start()

        @pl.when(is_top | is_bottom)
        def _():
            lines = jnp.concatenate(
                [jnp.where(is_top, buf[f, 1].astype(F32), buf[f, rows].astype(F32)) for f in range(nf)], axis=0
            ).astype(BF16)
            spreads = jnp.dot(lines, spread[...], preferred_element_type=F32)
            for p in range(half):
                part_p = spreads[:, p * LANES : (p + 1) * LANES]
                for slot in range(slots):
                    faces_here = [f for f in range(nf) if f // 2 == slot]
                    first = faces_here[0]
                    packed = part_p[first * C : (first + 1) * C]
                    if len(faces_here) > 1:
                        packed = jnp.where(lane < 64, packed, turn(part_p[(first + 1) * C : (first + 2) * C], 64))
                    ns_out[k, p, slot] = packed.astype(BF16)
            packs[k][ns_slot()] = ns_out[k, 0]
            for t in range(tiles):
                same, across = ns_copies(k, t)

                @pl.when(tile != t)
                def _():
                    same.start()

                across.start()

        up, down = halo_copies(k, buf)

        @pl.when(jnp.logical_not(is_top))
        def _():
            up.start()

        @pl.when(jnp.logical_not(is_bottom))
        def _():
            down.start()

    def not_own_ns(i):
        n, which = divmod(i - 3, 2)
        if which:
            return jnp.bool_(True)
        return jnp.logical_not(is_top if n == 0 else is_bottom)

    def forward_exchange(k):
        for i, slot in enumerate(forward_slots()):
            fwd = forward_copy(k, i, slot)
            if i < 3:
                fwd.wait_recv()
            else:

                @pl.when(not_own_ns(i))
                def _():
                    fwd.wait_recv()

            fwd.start()

    def link(f, e):
        base = ((face * nf + f) * EDGES + e) * 3
        return links[base], links[base + 1], links[base + 2]

    def source(k, f, e):
        g, e2, flip = link(f, e)
        q2, f2 = lax.div(g, nf), lax.rem(g, nf)
        we = lax.div(e2, 2)
        idx = we * (flip * faces_axis + q2) + (1 - we) * (ns_base + e2 * faces_axis + q2)
        other = upper_half + flip - 2 * upper_half * flip
        bit = we * (3 - e2) + (1 - we) * (1 - other)
        start = 64 * lax.rem(f2, 2) + bit + flip * 2 * (rows - 1)
        return packs[k][idx, lax.div(f2, 2)], start, 2 - 4 * flip

    def pick(k):
        for slot in arriving_slots():
            copy(packs[k].at[slot], packs[k].at[slot], s_fwd.at[k, 0], r_packs.at[k, slot], (sibling, tile)).wait_recv()
        d = lax.broadcasted_iota(jnp.int32, (1, LANES), 1)
        west_r = d // 2
        west_ok = (d % 2 == 0) & (d < 2 * rows)
        east_r = ((d + 1) % LANES) // 2
        east_ok = (d % 2 == 1) & (east_r < rows)
        for f in range(nf):
            ws, wstart, wstep = source(k, f, 2)
            es, estart, estep = source(k, f, 3)
            places = jnp.concatenate(
                [
                    one_hot(LANES, jnp.where(west_ok, wstart + wstep * west_r, -1)),
                    one_hot(LANES, jnp.where(east_ok, estart + estep * east_r, -1)),
                ],
                axis=0,
            )
            gp[k, f] = jnp.dot(
                jnp.concatenate([ws, es], axis=1), places, preferred_element_type=F32
            ).astype(BF16)
        for e in range(2):
            srcs, places = [], []
            for f in range(nf):
                s, start, step = source(k, f, e)
                ok = (d >= f * rows) & (d < (f + 1) * rows)
                srcs.append(s)
                places.append(one_hot(LANES, jnp.where(ok, start + step * (d - f * rows), -1)))
            seg_out[k, e] = jnp.dot(
                jnp.concatenate(srcs, axis=1), jnp.concatenate(places, axis=0), preferred_element_type=F32
            ).astype(BF16)
        up, down = ends_copies(k)
        to_top, to_bottom = seg_copies(k)

        @pl.when(is_top)
        def _():
            seg_in[k, 0] = seg_out[k, 0]

        @pl.when(is_bottom)
        def _():
            seg_in[k, last] = seg_out[k, 1]

        @pl.when(jnp.logical_not(is_top))
        def _():
            to_top.start()
            up.start()

        @pl.when(jnp.logical_not(is_bottom))
        def _():
            to_bottom.start()
            down.start()

        for f in range(nf):
            full[k, f] = gp[k, f].astype(F32)

    def stack3(a, first):
        return [turn(a, first), a, turn(a, -first)]

    def columns_forward(k, which):
        w = wst_ref[which]
        for f in range(nf):
            stacked = jnp.concatenate(stack3(full[k, f], 2), axis=0).astype(BF16)
            y = jnp.dot(w, stacked, preferred_element_type=F32)
            addcol[f] = jnp.where(even, y[:C], y[2 * C :])

    def end_rules(f, e):
        g, e2, flip = link(f, e)
        we = lax.div(e2, 2)
        first = rules[g * EDGES + we * (e2 - 2) + (1 - we) * 2 * e2]
        final = rules[g * EDGES + we * e2 + (1 - we) * (1 + 2 * e2)]
        first = jnp.where(first == we, 1.0, 0.0)
        final = jnp.where(final == we, 1.0, 0.0)
        low = jnp.where(flip == 0, first, final)
        high = jnp.where(flip == 0, final, first)
        return e2 * 2 + flip, low, high

    def columns_backward(k, which):
        for f in range(nf):
            wu, wlow, whigh = end_rules(f, 2)
            eu, elow, ehigh = end_rules(f, 3)
            a = full[k, f]
            low = jnp.where(lane == 0, wlow, jnp.where(lane == LANES - 1, elow, 0.0)) * top_f
            high = jnp.where(lane == 2 * rows - 2, whigh, jnp.where(lane == 2 * rows - 3, ehigh, 0.0)) * bottom_f
            stacked = jnp.concatenate(stack3(a, -2) + [a * low, a * high], axis=0).astype(BF16)
            weights = jnp.concatenate([u_ref[which, wu], u_ref[which, eu]], axis=0)
            y = jnp.dot(weights, stacked, preferred_element_type=F32)
            addcol[f] = jnp.where(even, y[:C], y[C:]).astype(BF16).astype(F32)

    def finish_ends(k, buf, which, forward):
        above = (lane == LANES - 2) | (lane == LANES - 3)
        below = (lane == 2 * rows) | (lane == 2 * rows - 1)

        @pl.when(jnp.logical_not(is_top))
        def _():
            copy(gpn.at[k, 0], gpn.at[k, 0], s_ends.at[k, 0], r_ends.at[k, 0], (face, tile - 1)).wait_recv()
            copy(buf.at[:, 0], buf.at[:, 0], s_halo.at[k, 0], r_halo.at[k, 0], (face, tile - 1)).wait_recv()
            for f in range(nf):
                full[k, f] = jnp.where(above, turn(gpn[k, 0, f].astype(F32), -2 * rows), full[k, f])

        @pl.when(jnp.logical_not(is_bottom))
        def _():
            copy(gpn.at[k, 1], gpn.at[k, 1], s_ends.at[k, 1], r_ends.at[k, 1], (face, tile + 1)).wait_recv()
            hup_ref = buf.at[:, rows + 1]
            copy(hup_ref, hup_ref, s_halo.at[k, 1], r_halo.at[k, 1], (face, tile + 1)).wait_recv()
            for f in range(nf):
                full[k, f] = jnp.where(below, turn(gpn[k, 1, f].astype(F32), 2 * rows), full[k, f])

        def assemble(e):
            for t in range(tiles):

                @pl.when(tile != t)
                def _():
                    ref = seg_in.at[k, t]
                    copy(ref, ref, s_seg.at[k, 0], r_seg.at[k, t], (face, last - tile)).wait_recv()

            for f in range(nf):
                for i in range(width // LANES):
                    piece = jnp.zeros((C, LANES), F32)
                    for t in range(tiles):
                        if t * rows // LANES == i:
                            off = t * rows % LANES
                            moved = turn(seg_in[k, t].astype(F32), off - f * rows)
                            piece = jnp.where((lane >= off) & (lane < off + rows), moved, piece)
                    line_in[f, :, i * LANES : (i + 1) * LANES] = piece

            if forward:
                row = 0 if e == 0 else rows + 1
                for f in range(nf):
                    line = line_in[f]
                    buf[f, row] = line.astype(BF16)
                    ghost = full[k, f]
                    mixed = jnp.where(lane == LANES - 1, line[:, -LANES:], line[:, :LANES])
                    base = (face * nf + f) * EDGES + 2 * e
                    by_line_w = rules[base] == 0
                    by_line_e = rules[base + 1] == 0
                    if e == 0:
                        from_line, from_col = turn(mixed, -2), turn(ghost, -2)
                        at_w, at_e = LANES - 2, LANES - 3
                    else:
                        from_line, from_col = turn(mixed, 2 * rows), turn(ghost, 2)
                        at_w, at_e = 2 * rows, 2 * rows - 1
                    corner_w = jnp.where(by_line_w, from_line, from_col)
                    corner_e = jnp.where(by_line_e, from_line, from_col)
                    full[k, f] = jnp.where(lane == at_w, corner_w, jnp.where(lane == at_e, corner_e, ghost))
            else:
                row = 0 if e == 0 else rows + 1
                wide = lax.broadcasted_iota(jnp.int32, (C, width), 1)
                for f in range(nf):
                    buf[f, row] = jnp.zeros((C, width), BF16)
                    u, low, high = end_rules(f, e)
                    line = line_in[f]
                    ahead = jnp.where(wide == width - 1, 0.0, pltpu.roll(line, width - 1, 1))
                    behind = jnp.where(wide == 0, 0.0, pltpu.roll(line, 1, 1))
                    ends = [
                        line * jnp.where(wide == 0, low, 0.0), line * jnp.where(wide == width - 1, high, 0.0)
                    ]
                    stacked = jnp.concatenate([ahead, line, behind] + ends, axis=0).astype(BF16)
                    y = jnp.dot(u_ref[which, u], stacked, preferred_element_type=F32)
                    addrow[e, f] = y.astype(BF16).astype(F32)

        @pl.when(is_top)
        def _():
            assemble(0)

        @pl.when(is_bottom)
        def _():
            assemble(1)

    def conv_row(w, buf, f, r, ghost):
        y = jnp.dot(w, buf[f, pl.ds(r, 3)].reshape(3 * C, width), preferred_element_type=F32)
        first, final = lane == 0, lane == LANES - 1
        ins = turn(ghost, -2 * r)
        parts = width // LANES
        cut = lambda a, i: a[:, i * LANES : (i + 1) * LANES]
        west = [turn(cut(y[:C], i), 1) for i in range(parts)]
        east = [turn(cut(y[2 * C :], i), -1) for i in range(parts)]
        out = []
        for i in range(parts):
            left = jnp.where(first, west[i - 1] if i > 0 else ins, west[i])
            right = jnp.where(final, east[i + 1] if i < parts - 1 else ins, east[i])
            out.append(cut(y[C : 2 * C], i) + left + right)
        return out

    def run_rows(which, buf, rs, finish, fresh):
        def face_step(f, carry):
            w = wst_ref[which]
            ghost = addcol[f]
            acc = jnp.zeros((C, LANES), F32) if fresh else cp[f]
            for r in rs:
                total = conv_row(w, buf, f, r, ghost)
                kept = finish(f, r, total)
                if kept is not None:
                    acc = keep(acc, r, kept[0], kept[-1])
            if finish is not finish_last:
                cp[f] = acc
            return carry

        lax.fori_loop(0, nf, face_step, 0)

    def put(ref, f, r, parts, dtype):
        ref[f, r] = jnp.concatenate([p.astype(dtype) for p in parts], axis=1)

    def bias(i):
        return jnp.broadcast_to(b_ref[i], (C, LANES))

    def finish_first(f, r, total):
        pairs = [gelu_pair(p + bias(0)) for p in total]
        values = [p[0] for p in pairs]
        put(slope_ref, f, r, [p[1] for p in pairs], F32)
        put(hb, f, r + 1, values, BF16)
        return values

    def finish_second(f, r, total):
        pairs = [gelu_pair(p + bias(1)) for p in total]
        put(rowsb, f, r, [p[0] for p in pairs], BF16)
        og = ogb[f, r].astype(F32)
        grads = [og[:, i * LANES : (i + 1) * LANES] * p[1] for i, p in enumerate(pairs)]
        put(g2b, f, r + 1, grads, BF16)
        return grads

    def with_row(f, r, total):
        if r not in (0, rows - 1):
            return total
        e = 0 if r == 0 else 1
        return [p + addrow[e, f, :, i * LANES : (i + 1) * LANES] for i, p in enumerate(total)]

    def finish_third(f, r, total):
        total = with_row(f, r, total)
        slope = slope_ref[f, r]
        grads = [p * slope[:, i * LANES : (i + 1) * LANES] for i, p in enumerate(total)]
        put(g1b, f, r + 1, grads, BF16)
        return grads

    def finish_last(f, r, total):
        put(rowsb, f, r, with_row(f, r, total), BF16)
        return None

    def weight_products(i, grad_buf, field_buf, k):
        part[i] = jnp.zeros_like(part[i])
        ones = jnp.ones((16, width), BF16)

        def face_step(f, carry):
            first, final = lane == 0, lane == LANES - 1
            zero = jnp.zeros((C, LANES), F32)
            lefts, rights = [], []
            for r in range(rows):
                grad = grad_buf[f, r + 1]
                wide = grad.astype(F32)
                cuts = [wide[:, j : j + LANES] for j in range(0, width, LANES)]
                ahead = [turn(a, -1) for a in cuts]
                behind = [turn(a, 1) for a in cuts]
                n = len(cuts)
                shift_a = [jnp.where(final, ahead[j + 1] if j < n - 1 else zero, ahead[j]) for j in range(n)]
                shift_b = [jnp.where(first, behind[j - 1] if j > 0 else zero, behind[j]) for j in range(n)]
                lefts.append(
                    jnp.concatenate(
                        [
                            jnp.concatenate([a.astype(BF16) for a in shift_a], axis=1),
                            grad,
                            jnp.concatenate([b.astype(BF16) for b in shift_b], axis=1),
                        ],
                        axis=0,
                    )
                )
                rights.append(
                    jnp.concatenate([field_buf[f, pl.ds(r, 3)].reshape(3 * C, width), ones], axis=0)
                )
            inside = (lane < 2 * rows - 1) | (lane == LANES - 1)
            edge = jnp.where(inside, cp[f], 0.0)
            lefts.append(
                jnp.concatenate([jnp.where(even, edge, 0.0), zero, jnp.where(even, 0.0, edge)], axis=0).astype(BF16)
            )
            rights.append(
                jnp.concatenate(stack3(full[k, f], 2) + [jnp.zeros((16, LANES), F32)], axis=0).astype(BF16)
            )
            products = lax.dot_general(
                jnp.concatenate(lefts, axis=1),
                jnp.concatenate(rights, axis=1),
                (((1,), (1,)), ((), ())),
                preferred_element_type=F32,
            )
            part[i, :, : 3 * C + 16] += products
            return carry

        lax.fori_loop(0, nf, face_step, 0)

    block = 16
    per = 3 * C // block
    owners = 2 * per

    def block_of(ref, o):
        return ref.at[o // per, pl.ds(o % per * block, block)]

    def sum_copy(o):
        return copy(block_of(part, o), landed.at[me], s_sum.at[o], r_sum.at[me], (o // tiles, o % tiles))

    def start_sums():
        for o in range(owners):
            c = sum_copy(o)

            @pl.when(me != o)
            def _():
                c.start()

    def result_copy(o, j):
        ref = block_of(gw_ref, o)
        return copy(ref, ref, s_res.at[j], r_res.at[o], at(j))

    def add_sums():
        for o in range(owners):

            @pl.when(me == o)
            def _():
                landed[o] = block_of(part, o)[...]
                each_other(
                    lambda j: copy(landed.at[j], landed.at[j], s_sum.at[0], r_sum.at[j], at(j)).wait_recv()
                )
                total = lax.fori_loop(
                    1, n_dev, lambda j, t: t + landed[j], landed[0]
                )
                block_of(gw_ref, o)[...] = total
                each_other(lambda j: result_copy(o, j).start())

    to_rows(x_ref, xb, 1)

    def first_columns(f, carry):
        acc = jnp.zeros((C, LANES), F32)
        for r in range(rows):
            row = xb[f, r + 1].astype(F32)
            acc = keep(acc, r, row[:, :LANES], row[:, -LANES:])
        cp[f] = acc
        return carry

    lax.fori_loop(0, nf, first_columns, 0)
    d = lax.broadcasted_iota(jnp.int32, (1, LANES), 1)
    for p in range(half):
        seg = jnp.where(d % 2 == 1, p, last - p)
        target = jnp.where(d < 2 * rows, seg * rows + d // 2, -1)
        spread[:, p * LANES : (p + 1) * LANES] = one_hot(width, target)
    addrow[...] = jnp.zeros_like(addrow)
    pl.semaphore_wait(barrier, n_dev - 1)

    inner = list(range(1, rows - 1))
    outer = [0, rows - 1]

    start_exchange(0, xb)
    to_rows(og_ref, ogb, 0)
    forward_exchange(0)
    pick(0)
    columns_forward(0, 0)
    run_rows(0, xb, inner, finish_first, True)
    finish_ends(0, xb, None, True)
    columns_forward(0, 0)
    run_rows(0, xb, outer, finish_first, False)

    start_exchange(1, hb)
    forward_exchange(1)
    pick(1)
    columns_forward(1, 1)
    run_rows(1, hb, inner, finish_second, True)
    finish_ends(1, hb, None, True)
    columns_forward(1, 1)
    run_rows(1, hb, outer, finish_second, False)

    start_exchange(2, g2b)
    weight_products(0, g2b, hb, 1)
    from_rows(rowsb, out_ref)
    forward_exchange(2)
    pick(2)
    columns_backward(2, 0)
    run_rows(2, g2b, inner, finish_third, True)
    finish_ends(2, g2b, 0, False)
    columns_backward(2, 0)
    run_rows(2, g2b, outer, finish_third, False)

    start_exchange(3, g1b)
    weight_products(1, g1b, xb, 0)
    start_sums()
    forward_exchange(3)
    pick(3)
    columns_backward(3, 1)
    run_rows(3, g1b, inner, finish_last, True)
    add_sums()
    finish_ends(3, g1b, 1, False)
    columns_backward(3, 1)
    run_rows(3, g1b, outer, finish_last, False)
    from_rows(rowsb, gf_ref)

    for o in range(owners):

        @pl.when(me != o)
        def _():
            result_copy(o, me).wait_recv()
            sum_copy(o).wait_send()

        @pl.when(me == o)
        def _():
            each_other(lambda j: result_copy(o, j).wait_send())

    for k, buf in enumerate((xb, hb, g2b, g1b)):
        for c in direct_copies(k):
            c.wait_send()
        for i, slot in enumerate(forward_slots()):
            forward_copy(k, i, slot).wait_send()
        ups = (halo_copies(k, buf)[0], ends_copies(k)[0], seg_copies(k)[0])
        downs = (halo_copies(k, buf)[1], ends_copies(k)[1], seg_copies(k)[1])

        @pl.when(jnp.logical_not(is_top))
        def _():
            for c in ups:
                c.wait_send()

        @pl.when(jnp.logical_not(is_bottom))
        def _():
            for c in downs:
                c.wait_send()

        @pl.when(is_top | is_bottom)
        def _():
            for t in range(tiles):
                same, across = ns_copies(k, t)

                @pl.when(tile != t)
                def _():
                    same.wait_send()

                across.wait_send()


def body(field_in, out_grad, weight_first, bias_first, weight_second, bias_second, face_links, corner_rules):
    faces_axis, tiles = lax.axis_size("face"), lax.axis_size("tile")
    nf, C, rows, width = field_in.shape
    n_dev = faces_axis * tiles
    ahead = lambda w: jnp.transpose(w, (3, 0, 2, 1)).reshape(3 * C, 3 * C)
    behind = lambda w: jnp.transpose(w[:, :, ::-1, ::-1], (3, 1, 2, 0)).reshape(3 * C, 3 * C)
    stacks = jnp.stack([ahead(weight_first), ahead(weight_second), behind(weight_second), behind(weight_first)])

    def line_weights(w):
        taps = []
        for line in (w[:, :, 0, :], w[:, :, 2, :], w[:, :, :, 0], w[:, :, :, 2]):
            for turned in (line, line[:, :, ::-1]):
                five = jnp.concatenate([turned, turned[:, :, :1], turned[:, :, 2:]], axis=2)
                taps.append(jnp.transpose(five, (1, 2, 0)).reshape(C, 5 * C))
        return jnp.stack(taps)

    lines = jnp.stack([line_weights(weight_second), line_weights(weight_first)])
    biases = jnp.stack([bias_first, bias_second])[:, :, None]
    slots = (nf + 1) // 2
    vm = pltpu.VMEM
    dma = pltpu.SemaphoreType.DMA
    padded = vm((nf, rows + 2, C, width), BF16)
    scratch = [
        padded, padded, padded, padded,
        vm((nf, rows, C, width), BF16),
        vm((nf, rows, C, width), BF16),
        vm((nf, rows, C, width), F32),
        vm((nf, C, LANES), F32),
        *[vm((4 * faces_axis, slots, C, LANES), BF16)] * 4,
        vm((4, nf, C, LANES), BF16),
        vm((4, 2, nf, C, LANES), BF16),
        vm((4, nf, C, LANES), F32),
        vm((4, 2, C, LANES), BF16),
        vm((4, tiles, C, LANES), BF16),
        vm((nf, C, width), F32),
        vm((4, tiles // 2, slots, C, LANES), BF16),
        vm((width, tiles // 2 * LANES), BF16),
        vm((nf, C, LANES), F32),
        vm((2, nf, C, width), F32),
        vm((2, 3 * C, 2 * LANES), F32),
        vm((n_dev, 16, 2 * LANES), F32),
        dma((4, 2)), dma((4, 2)), dma((4, 4)), dma((4, 7)), dma((4, 2 * tiles)), dma((4, 4 * faces_axis)),
        dma((4, 2)), dma((4, 2)), dma((4, 2)), dma((4, tiles)),
        dma((2 * 3 * C // 16,)), dma((n_dev,)), dma((n_dev,)), dma((2 * 3 * C // 16,)),
    ]
    vmem = pl.BlockSpec(memory_space=pltpu.VMEM)
    smem = pl.BlockSpec(memory_space=pltpu.SMEM)
    flops = 2 * 6 * 9 * C * C * nf * rows * width
    output, grad_field, sums = pl.pallas_call(
        functools.partial(fused_kernel, faces_axis, tiles),
        in_specs=[smem, smem] + [vmem] * 5,
        out_specs=[vmem] * 3,
        out_shape=[
            jax.ShapeDtypeStruct(field_in.shape, BF16),
            jax.ShapeDtypeStruct(field_in.shape, BF16),
            jax.ShapeDtypeStruct((2, 3 * C, 2 * LANES), F32),
        ],
        scratch_shapes=scratch,
        compiler_params=pltpu.CompilerParams(vmem_limit_bytes=56 << 20, collective_id=0, has_side_effects=True),
        cost_estimate=pl.CostEstimate(flops=flops, bytes_accessed=10**7, transcendentals=5 * 10**6),
    )(face_links.reshape(-1), corner_rules.reshape(-1), field_in, out_grad, stacks, biases, lines)
    shaped = lambda g: jnp.transpose(g[:, : 3 * C].reshape(3, C, 3, C), (1, 3, 2, 0)) / width
    middle = lambda g: g[C : 2 * C, 3 * C] / width
    return output, grad_field, shaped(sums[1]), middle(sums[1]), shaped(sums[0]), middle(sums[0])


def solution(mesh):
    cells = P("face", None, "tile", None)
    return jax.shard_map(
        body,
        mesh=mesh,
        in_specs=(cells, cells, P(), P(), P(), P(), P(), P()),
        out_specs=(cells, cells, P(), P(), P(), P()),
        check_vma=False,
    )
```

```python
import functools

import jax
import jax.numpy as jnp
from jax import lax
from jax.experimental import pallas as pl
from jax.experimental.pallas import tpu as pltpu
from jax.sharding import PartitionSpec as P

INV_ROOT_TWO = 0.7071067811865476
INV_ROOT_TWO_PI = 0.3989422804014327
F32 = jnp.float32
BF16 = jnp.bfloat16
LANES = 128
MESH_ID = pl.DeviceIdType.MESH
EDGES = 4
GROUP = 16


def gelu_pair(values):
    normal_cdf = 0.5 * (1.0 + lax.erf(values * INV_ROOT_TWO))
    normal_pdf = jnp.exp(-0.5 * values * values) * INV_ROOT_TWO_PI
    return (values * normal_cdf, normal_cdf + values * normal_pdf)


def one_hot(rows, target):
    row = lax.broadcasted_iota(jnp.int32, (rows, target.shape[1]), 0)
    return jnp.where(row == target, 1.0, 0.0).astype(BF16)


def turn(a, shift):
    return pltpu.roll(a, shift % LANES, 1)


def from_rows(src, dst, only=None):
    nf, rows, C, _ = src.shape
    for f in range(nf) if only is None else only:
        for r0 in range(0, rows, GROUP):
            n = min(GROUP, rows - r0)
            for c0 in range(0, C, GROUP):
                block = src[f, r0 : r0 + n, c0 : c0 + GROUP]
                if n < GROUP:
                    block = jnp.swapaxes(block.astype(F32), 0, 1).astype(BF16)
                else:
                    block = jnp.swapaxes(block, 0, 1)
                dst[f, c0 : c0 + GROUP, r0 : r0 + n] = block


def fused_kernel(
    faces_axis, tiles, links, rules, x_hbm, og_hbm, w1_hbm, w2_hbm, b1_hbm, b2_hbm,
    out_hbm, gf_hbm, gw_ref,
    x_ref, og_ref, w1_ref, w2_ref, b1_ref, b2_ref, s_in, s_out, pre_ref, we_place, ns_place,
    wst_ref, u_ref, b_ref,
    xb, hb, g2b, g1b, ogb, rowsb, slope_ref, cp, packs0, packs1, packs2, packs3, gp, gpn, full, seg_out, seg_in, line_in, ns_out, spread,
    addcol, addrow, part, landed,
    s_halo, r_halo, s_direct, s_fwd, s_ns, r_packs, s_ends, r_ends, s_seg, r_seg, s_sum, r_sum, s_res, r_res,
):
    nf, C, rows, width = x_ref.shape
    packs = (packs0, packs1, packs2, packs3)
    slots = packs0.shape[1]
    n_dev = faces_axis * tiles
    face = lax.axis_index("face")
    tile = lax.axis_index("tile")
    me = face * tiles + tile
    last = tiles - 1
    mirror_tile = last - tile
    half = tiles // 2
    lane = lax.broadcasted_iota(jnp.int32, (C, LANES), 1)
    even = lane % 2 == 0
    is_top = tile == 0
    is_bottom = tile == last
    top_f = jnp.where(is_top, 1.0, 0.0)
    bottom_f = jnp.where(is_bottom, 1.0, 0.0)
    upper_half = jnp.where(tile >= half, 1, 0)
    peer = lax.rem(face + 2, faces_axis)
    sibling = face + 1 - 2 * lax.rem(face, 2)
    sibling_peer = lax.rem(sibling + 2, faces_axis)

    def at(j):
        return (lax.div(j, tiles), lax.rem(j, tiles))

    def each_other(body):
        def step(j, carry):
            @pl.when(j != me)
            def _():
                body(j)

            return carry

        lax.fori_loop(0, n_dev, step, 0)

    barrier = pltpu.get_barrier_semaphore()
    each_other(lambda j: pl.semaphore_signal(barrier, inc=1, device_id=at(j), device_id_type=MESH_ID))

    inputs = [
        pltpu.make_async_copy(src, dst, s_in.at[i])
        for i, (src, dst) in enumerate(
            (
                (x_hbm, x_ref), (w1_hbm, w1_ref), (w2_hbm, w2_ref), (b1_hbm, b1_ref), (b2_hbm, b2_ref),
                (og_hbm, og_ref),
            )
        )
    ]
    for c in inputs:
        c.start()

    def to_rows(src, dst, first):
        for f in range(nf):
            for r0 in range(0, rows, GROUP):
                n = min(GROUP, rows - r0)
                for c0 in range(0, C, GROUP):
                    block = src[f, c0 : c0 + GROUP, r0 : r0 + n]
                    if n < GROUP:
                        block = jnp.swapaxes(block.astype(F32), 0, 1).astype(BF16)
                    else:
                        block = jnp.swapaxes(block, 0, 1)
                    dst[f, first + r0 : first + r0 + n, c0 : c0 + GROUP] = block

    def keep(acc, r, lo, hi):
        mixed = turn(jnp.where(lane == LANES - 1, hi, lo), 2 * r)
        return jnp.where((lane == 2 * r) | (lane == (2 * r - 1) % LANES), mixed, acc)

    def copy(src, dst, send, recv, device):
        return pltpu.make_async_remote_copy(src, dst, send, recv, device, MESH_ID)

    ns_base = 2 * faces_axis

    def halo_copies(k, buf):
        up = copy(buf.at[:, 1], buf.at[:, rows + 1], s_halo.at[k, 0], r_halo.at[k, 1], (face, tile - 1))
        down = copy(buf.at[:, rows], buf.at[:, 0], s_halo.at[k, 1], r_halo.at[k, 0], (face, tile + 1))
        return up, down

    def direct_copies(k):
        own = packs[k].at[face]
        here = face
        there = faces_axis + face
        return [
            copy(own, packs[k].at[there], s_direct.at[k, 0], r_packs.at[k, there], (face, mirror_tile)),
            copy(own, packs[k].at[there], s_direct.at[k, 1], r_packs.at[k, there], (peer, mirror_tile)),
            copy(own, packs[k].at[here], s_direct.at[k, 2], r_packs.at[k, here], (peer, tile)),
            copy(own, packs[k].at[here], s_direct.at[k, 3], r_packs.at[k, here], (sibling, tile)),
        ]

    def ns_slot():
        return ns_base + jnp.where(is_top, 0, 1) * faces_axis + face

    def ns_copies(k, j):
        t = jnp.where(is_top, last - j, j)
        src = ns_out.at[k, min(j, last - j)]
        slot = ns_slot()
        return [
            copy(src, packs[k].at[slot], s_ns.at[k, j], r_packs.at[k, slot], (face, t)),
            copy(src, packs[k].at[slot], s_ns.at[k, tiles + j], r_packs.at[k, slot], (peer, t)),
        ]

    def forward_slots():
        return [faces_axis + face, peer, faces_axis + peer] + [
            ns_base + n * faces_axis + q for n in range(2) for q in (face, peer)
        ]

    def arriving_slots():
        return [sibling, faces_axis + sibling, sibling_peer, faces_axis + sibling_peer] + [
            ns_base + n * faces_axis + q for n in range(2) for q in (sibling, sibling_peer)
        ]

    def forward_copy(k, i, slot):
        ref = packs[k].at[slot]
        return copy(ref, ref, s_fwd.at[k, i], r_packs.at[k, slot], (sibling, tile))

    def ends_copies(k):
        return (
            copy(gp.at[k], gpn.at[k, 1], s_ends.at[k, 0], r_ends.at[k, 1], (face, tile - 1)),
            copy(gp.at[k], gpn.at[k, 0], s_ends.at[k, 1], r_ends.at[k, 0], (face, tile + 1)),
        )

    def seg_copies(k):
        dst = seg_in.at[k, tile]
        return (
            copy(seg_out.at[k, 0], dst, s_seg.at[k, 0], r_seg.at[k, tile], (face, 0)),
            copy(seg_out.at[k, 1], dst, s_seg.at[k, 1], r_seg.at[k, tile], (face, last)),
        )

    def start_exchange(k, buf):
        for slot in range(slots):
            faces_here = [f for f in range(nf) if f // 2 == slot]
            packed = turn(cp[faces_here[0]], 1)
            if len(faces_here) > 1:
                packed = jnp.where(lane < 64, packed, turn(cp[faces_here[1]], 65))
            packs[k][face, slot] = packed.astype(BF16)
        @pl.when(is_top | is_bottom)
        def _():
            lines = jnp.concatenate(
                [jnp.where(is_top, buf[f, 1].astype(F32), buf[f, rows].astype(F32)) for f in range(nf)], axis=0
            ).astype(BF16)
            spreads = jnp.dot(lines, spread[...], preferred_element_type=F32)
            for p in range(half):
                part_p = spreads[:, p * LANES : (p + 1) * LANES]
                for slot in range(slots):
                    faces_here = [f for f in range(nf) if f // 2 == slot]
                    first = faces_here[0]
                    packed = part_p[first * C : (first + 1) * C]
                    if len(faces_here) > 1:
                        packed = jnp.where(lane < 64, packed, turn(part_p[(first + 1) * C : (first + 2) * C], 64))
                    ns_out[k, p, slot] = packed.astype(BF16)
            packs[k][ns_slot()] = ns_out[k, 0]
            for j in range(tiles):
                same, across = ns_copies(k, j)
                across.start()
                if j < last:
                    same.start()

        for c in direct_copies(k):
            c.start()
        up, down = halo_copies(k, buf)

        @pl.when(jnp.logical_not(is_top))
        def _():
            up.start()

        @pl.when(jnp.logical_not(is_bottom))
        def _():
            down.start()

    def not_own_ns(i):
        n, which = divmod(i - 3, 2)
        if which:
            return jnp.bool_(True)
        return jnp.logical_not(is_top if n == 0 else is_bottom)

    def forward_exchange(k):
        for i, slot in enumerate(forward_slots()):
            fwd = forward_copy(k, i, slot)
            if i < 3:
                fwd.wait_recv()
            else:

                @pl.when(not_own_ns(i))
                def _():
                    fwd.wait_recv()

            fwd.start()

    def link(f, e):
        return links[0, e, face * nf + f], links[1, e, face * nf + f], links[2, e, face * nf + f]

    def source(f, e):
        g, e2, flip = link(f, e)
        q2, f2 = lax.div(g, nf), lax.rem(g, nf)
        we = lax.div(e2, 2)
        idx = we * (flip * faces_axis + q2) + (1 - we) * (ns_base + e2 * faces_axis + q2)
        return idx, lax.div(f2, 2)

    def source_lanes(f, e):
        g, e2, flip = link(f, e)
        we = lax.div(e2, 2)
        other = upper_half + flip - 2 * upper_half * flip
        bit = we * (3 - e2) + (1 - we) * (1 - other)
        return 64 * lax.rem(lax.rem(g, nf), 2) + bit + flip * 2 * (rows - 1), 2 - 4 * flip

    def place_sources():
        d = lax.broadcasted_iota(jnp.int32, (1, LANES), 1)
        west_r = d // 2
        west_ok = (d % 2 == 0) & (d < 2 * rows)
        east_r = ((d + 1) % LANES) // 2
        east_ok = (d % 2 == 1) & (east_r < rows)
        for f in range(nf):
            for j, (e, ok, r) in enumerate(((2, west_ok, west_r), (3, east_ok, east_r))):
                start, step = source_lanes(f, e)
                we_place[f, j * LANES : (j + 1) * LANES] = one_hot(LANES, jnp.where(ok, start + step * r, -1))
            ok = (d >= f * rows) & (d < (f + 1) * rows)
            for e in range(2):
                start, step = source_lanes(f, e)
                ns_place[e, f * LANES : (f + 1) * LANES] = one_hot(
                    LANES, jnp.where(ok, start + step * (d - f * rows), -1)
                )

    def pick(k):
        for slot in arriving_slots():
            copy(packs[k].at[slot], packs[k].at[slot], s_fwd.at[k, 0], r_packs.at[k, slot], (sibling, tile)).wait_recv()

        def taken(f, e):
            idx, slot = source(f, e)
            return packs[k][idx, slot]

        for e in range(2):
            srcs = jnp.concatenate([taken(f, e) for f in range(nf)], axis=1)
            seg_out[k, e] = jnp.dot(srcs, ns_place[e], preferred_element_type=F32).astype(BF16)
        for f in range(nf):
            srcs = jnp.concatenate([taken(f, 2), taken(f, 3)], axis=1)
            gp[k, f] = jnp.dot(srcs, we_place[f], preferred_element_type=F32).astype(BF16)
        up, down = ends_copies(k)
        to_top, to_bottom = seg_copies(k)

        @pl.when(is_top)
        def _():
            seg_in[k, 0] = seg_out[k, 0]

        @pl.when(is_bottom)
        def _():
            seg_in[k, last] = seg_out[k, 1]

        @pl.when(jnp.logical_not(is_top))
        def _():
            to_top.start()
            up.start()

        @pl.when(jnp.logical_not(is_bottom))
        def _():
            to_bottom.start()
            down.start()

        for f in range(nf):
            full[k, f] = gp[k, f].astype(F32)

    def stack3(a, first):
        return [turn(a, first), a, turn(a, -first)]

    def columns_forward(k, which):
        w = wst_ref[which]
        for f in range(nf):
            stacked = jnp.concatenate(stack3(full[k, f], 2), axis=0).astype(BF16)
            y = jnp.dot(w, stacked, preferred_element_type=F32)
            addcol[f] = jnp.where(even, y[:C], y[2 * C :])

    def end_rules(f, e):
        g, e2, flip = link(f, e)
        we = lax.div(e2, 2)
        first = rules[we * (e2 - 2) + (1 - we) * 2 * e2, g]
        final = rules[we * e2 + (1 - we) * (1 + 2 * e2), g]
        first = jnp.where(first == we, 1.0, 0.0)
        final = jnp.where(final == we, 1.0, 0.0)
        low = jnp.where(flip == 0, first, final)
        high = jnp.where(flip == 0, final, first)
        return e2 * 2 + flip, low, high

    def columns_backward(k, which):
        for f in range(nf):
            wu, wlow, whigh = end_rules(f, 2)
            eu, elow, ehigh = end_rules(f, 3)
            a = full[k, f]
            low = jnp.where(lane == 0, wlow, jnp.where(lane == LANES - 1, elow, 0.0)) * top_f
            high = jnp.where(lane == 2 * rows - 2, whigh, jnp.where(lane == 2 * rows - 3, ehigh, 0.0)) * bottom_f
            stacked = jnp.concatenate(stack3(a, -2) + [a * low, a * high], axis=0).astype(BF16)
            weights = jnp.concatenate([u_ref[which, wu], u_ref[which, eu]], axis=0)
            y = jnp.dot(weights, stacked, preferred_element_type=F32)
            addcol[f] = jnp.where(even, y[:C], y[C:]).astype(BF16).astype(F32)

    def finish_ends(k, buf, which, forward):
        above = (lane == LANES - 2) | (lane == LANES - 3)
        below = (lane == 2 * rows) | (lane == 2 * rows - 1)

        @pl.when(jnp.logical_not(is_top))
        def _():
            copy(gpn.at[k, 0], gpn.at[k, 0], s_ends.at[k, 0], r_ends.at[k, 0], (face, tile - 1)).wait_recv()
            copy(buf.at[:, 0], buf.at[:, 0], s_halo.at[k, 0], r_halo.at[k, 0], (face, tile - 1)).wait_recv()
            for f in range(nf):
                full[k, f] = jnp.where(above, turn(gpn[k, 0, f].astype(F32), -2 * rows), full[k, f])

        @pl.when(jnp.logical_not(is_bottom))
        def _():
            copy(gpn.at[k, 1], gpn.at[k, 1], s_ends.at[k, 1], r_ends.at[k, 1], (face, tile + 1)).wait_recv()
            hup_ref = buf.at[:, rows + 1]
            copy(hup_ref, hup_ref, s_halo.at[k, 1], r_halo.at[k, 1], (face, tile + 1)).wait_recv()
            for f in range(nf):
                full[k, f] = jnp.where(below, turn(gpn[k, 1, f].astype(F32), 2 * rows), full[k, f])

        def assemble(e):
            for t in range(tiles):

                @pl.when(tile != t)
                def _():
                    ref = seg_in.at[k, t]
                    copy(ref, ref, s_seg.at[k, 0], r_seg.at[k, t], (face, last - tile)).wait_recv()

            for f in range(nf):
                for i in range(width // LANES):
                    piece = jnp.zeros((C, LANES), F32)
                    for t in range(tiles):
                        if t * rows // LANES == i:
                            off = t * rows % LANES
                            moved = turn(seg_in[k, t].astype(F32), off - f * rows)
                            piece = jnp.where((lane >= off) & (lane < off + rows), moved, piece)
                    line_in[f, :, i * LANES : (i + 1) * LANES] = piece

            if forward:
                row = 0 if e == 0 else rows + 1
                for f in range(nf):
                    line = line_in[f]
                    buf[f, row] = line.astype(BF16)
                    ghost = full[k, f]
                    mixed = jnp.where(lane == LANES - 1, line[:, -LANES:], line[:, :LANES])
                    by_line_w = rules[2 * e, face * nf + f] == 0
                    by_line_e = rules[2 * e + 1, face * nf + f] == 0
                    if e == 0:
                        from_line, from_col = turn(mixed, -2), turn(ghost, -2)
                        at_w, at_e = LANES - 2, LANES - 3
                    else:
                        from_line, from_col = turn(mixed, 2 * rows), turn(ghost, 2)
                        at_w, at_e = 2 * rows, 2 * rows - 1
                    corner_w = jnp.where(by_line_w, from_line, from_col)
                    corner_e = jnp.where(by_line_e, from_line, from_col)
                    full[k, f] = jnp.where(lane == at_w, corner_w, jnp.where(lane == at_e, corner_e, ghost))
            else:
                row = 0 if e == 0 else rows + 1
                wide = lax.broadcasted_iota(jnp.int32, (C, width), 1)
                for f in range(nf):
                    buf[f, row] = jnp.zeros((C, width), BF16)
                    u, low, high = end_rules(f, e)
                    line = line_in[f]
                    ahead = jnp.where(wide == width - 1, 0.0, pltpu.roll(line, width - 1, 1))
                    behind = jnp.where(wide == 0, 0.0, pltpu.roll(line, 1, 1))
                    ends = [
                        line * jnp.where(wide == 0, low, 0.0), line * jnp.where(wide == width - 1, high, 0.0)
                    ]
                    stacked = jnp.concatenate([ahead, line, behind] + ends, axis=0).astype(BF16)
                    y = jnp.dot(u_ref[which, u], stacked, preferred_element_type=F32)
                    addrow[e, f] = y.astype(BF16).astype(F32)

        @pl.when(is_top)
        def _():
            assemble(0)

        @pl.when(is_bottom)
        def _():
            assemble(1)

    def cut(a, i):
        return a[:, i * LANES : (i + 1) * LANES]

    def conv_row(w, buf, f, r, ins):
        y = jnp.dot(w, buf[f, pl.ds(r, 3)].reshape(3 * C, width), preferred_element_type=F32)
        first, final = lane == 0, lane == LANES - 1
        parts = width // LANES
        west = [turn(cut(y[:C], i), 1) for i in range(parts)]
        east = [turn(cut(y[2 * C :], i), -1) for i in range(parts)]
        out = []
        for i in range(parts):
            left = jnp.where(first, west[i - 1] if i > 0 else ins, west[i])
            right = jnp.where(final, east[i + 1] if i < parts - 1 else ins, east[i])
            out.append(cut(y[C : 2 * C], i) + left + right)
        return out

    def run_inner_products(which, buf):
        def face_step(f, carry):
            w = wst_ref[which]
            zero = jnp.zeros((C, LANES), F32)
            for r in range(1, rows - 1):
                for i, p in enumerate(conv_row(w, buf, f, r, zero)):
                    pre_ref[f, r, :, i * LANES : (i + 1) * LANES] = p
            return carry

        lax.fori_loop(0, nf, face_step, 0)

    def with_columns(f, r, ghost):
        ins = turn(ghost, -2 * r)
        total = [cut(pre_ref[f, r], i) for i in range(width // LANES)]
        total[0] = total[0] + jnp.where(lane == 0, ins, 0.0)
        total[-1] = total[-1] + jnp.where(lane == LANES - 1, ins, 0.0)
        return total

    def do_rows(which, buf, f, rs, finish, acc):
        ghost = addcol[f]
        for r in rs:
            if r in (0, rows - 1):
                total = conv_row(wst_ref[which], buf, f, r, turn(ghost, -2 * r))
            else:
                total = with_columns(f, r, ghost)
            kept = finish(f, r, total)
            if kept is not None:
                acc = keep(acc, r, kept[0], kept[-1])
        return acc

    def run_inner(which, buf, finish):
        def face_step(f, carry):
            cp[f] = do_rows(which, buf, f, range(1, rows - 1), finish, jnp.zeros((C, LANES), F32))
            return carry

        lax.fori_loop(0, nf, face_step, 0)

    def run_outer(which, buf, finish):
        accs = [do_rows(which, buf, f, (0, rows - 1), finish, cp[f]) for f in range(nf)]
        for f in range(nf):
            cp[f] = accs[f]

    def put(ref, f, r, parts, dtype):
        ref[f, r] = jnp.concatenate([p.astype(dtype) for p in parts], axis=1)

    def bias(i):
        return jnp.broadcast_to(b_ref[i], (C, LANES))

    def finish_first(f, r, total):
        pairs = [gelu_pair(p + bias(0)) for p in total]
        values = [p[0] for p in pairs]
        put(slope_ref, f, r, [p[1] for p in pairs], F32)
        put(hb, f, r + 1, values, BF16)
        return values

    def finish_second(f, r, total):
        pairs = [gelu_pair(p + bias(1)) for p in total]
        put(rowsb, f, r, [p[0] for p in pairs], BF16)
        og = ogb[f, r].astype(F32)
        grads = [og[:, i * LANES : (i + 1) * LANES] * p[1] for i, p in enumerate(pairs)]
        put(g2b, f, r + 1, grads, BF16)
        return grads

    def with_row(f, r, total):
        if r not in (0, rows - 1):
            return total
        e = 0 if r == 0 else 1
        return [p + addrow[e, f, :, i * LANES : (i + 1) * LANES] for i, p in enumerate(total)]

    def finish_third(f, r, total):
        total = with_row(f, r, total)
        slope = slope_ref[f, r]
        grads = [p * slope[:, i * LANES : (i + 1) * LANES] for i, p in enumerate(total)]
        put(g1b, f, r + 1, grads, BF16)
        return grads

    def finish_last(f, r, total):
        put(rowsb, f, r, with_row(f, r, total), BF16)
        return None

    def weight_products(i, grad_buf, field_buf, k):
        part[i] = jnp.zeros_like(part[i])
        ones = jnp.ones((16, width), BF16)

        def face_step(f, carry):
            first, final = lane == 0, lane == LANES - 1
            zero = jnp.zeros((C, LANES), F32)
            lefts, rights = [], []
            for r in range(rows):
                grad = grad_buf[f, r + 1]
                wide = grad.astype(F32)
                cuts = [wide[:, j : j + LANES] for j in range(0, width, LANES)]
                ahead = [turn(a, -1) for a in cuts]
                behind = [turn(a, 1) for a in cuts]
                n = len(cuts)
                shift_a = [jnp.where(final, ahead[j + 1] if j < n - 1 else zero, ahead[j]) for j in range(n)]
                shift_b = [jnp.where(first, behind[j - 1] if j > 0 else zero, behind[j]) for j in range(n)]
                lefts.append(
                    jnp.concatenate(
                        [
                            jnp.concatenate([a.astype(BF16) for a in shift_a], axis=1),
                            grad,
                            jnp.concatenate([b.astype(BF16) for b in shift_b], axis=1),
                        ],
                        axis=0,
                    )
                )
                rights.append(
                    jnp.concatenate([field_buf[f, pl.ds(r, 3)].reshape(3 * C, width), ones], axis=0)
                )
            inside = (lane < 2 * rows - 1) | (lane == LANES - 1)
            edge = jnp.where(inside, cp[f], 0.0)
            lefts.append(
                jnp.concatenate([jnp.where(even, edge, 0.0), zero, jnp.where(even, 0.0, edge)], axis=0).astype(BF16)
            )
            rights.append(
                jnp.concatenate(stack3(full[k, f], 2) + [jnp.zeros((16, LANES), F32)], axis=0).astype(BF16)
            )
            products = lax.dot_general(
                jnp.concatenate(lefts, axis=1),
                jnp.concatenate(rights, axis=1),
                (((1,), (1,)), ((), ())),
                preferred_element_type=F32,
            )
            part[i, :, : 3 * C + 16] += products
            return carry

        lax.fori_loop(0, nf, face_step, 0)

    block = 8
    per = 3 * C // block
    middle = max(tiles - 2, 1)

    def owner(i, o):
        j = o + 6 * i
        return (j // middle % faces_axis, 1 + j % middle)

    def is_owner(i, o):
        f, t = owner(i, o)
        return (face == f) & (tile == t)

    def block_of(ref, i, o):
        return ref.at[i, pl.ds(o * block, block)]

    def sum_copy(i, o):
        return copy(block_of(part, i, o), landed.at[i, me], s_sum.at[i, o], r_sum.at[i, me], owner(i, o))

    def start_sums(i):
        for o in range(per):
            c = sum_copy(i, o)

            @pl.when(jnp.logical_not(is_owner(i, o)))
            def _():
                c.start()

    def result_copy(i, o, j):
        ref = block_of(gw_ref, i, o)
        return copy(ref, ref, s_res.at[i, j], r_res.at[i, o], at(j))

    def add_sums(i):
        for o in range(per):

            @pl.when(is_owner(i, o))
            def _():
                each_other(
                    lambda j: copy(
                        landed.at[i, j], landed.at[i, j], s_sum.at[i, 0], r_sum.at[i, j], at(j)
                    ).wait_recv()
                )
                landed[i, me] = block_of(part, i, o)[...]
                total = lax.fori_loop(1, n_dev, lambda j, t: t + landed[i, j], landed[i, 0])
                block_of(gw_ref, i, o)[...] = total
                each_other(lambda j: result_copy(i, o, j).start())

    def place_weights():
        def blocks(count, places):
            row = lax.broadcasted_iota(jnp.int32, (C, count * C), 0)
            column = lax.broadcasted_iota(jnp.int32, (C, count * C), 1)
            hit = functools.reduce(jnp.logical_or, [column == row + p * C for p in places])
            return jnp.where(hit, 1.0, 0.0).astype(BF16)

        thirds = [blocks(3, [k]) for k in range(3)]
        straight = lambda a, e: jnp.dot(a, e, preferred_element_type=F32)
        turned = lambda a, e: lax.dot_general(a, e, (((0,), (0,)), ((), ())), preferred_element_type=F32)
        for which, w in ((0, w1_ref), (1, w2_ref)):
            for l in range(3):
                total = sum(straight(w[k, l], thirds[k]) for k in range(3))
                wst_ref[which, l * C : (l + 1) * C] = total.astype(BF16)
        for which, w in ((2, w2_ref), (3, w1_ref)):
            for l in range(3):
                total = sum(turned(w[2 - k, 2 - l], thirds[k]) for k in range(3))
                wst_ref[which, l * C : (l + 1) * C] = total.astype(BF16)
        row = lax.broadcasted_iota(jnp.int32, (C, C), 0)
        column = lax.broadcasted_iota(jnp.int32, (C, C), 1)
        for i, b in enumerate((b1_ref, b2_ref)):
            b_ref[i] = jnp.broadcast_to(
                jnp.sum(jnp.where(row == column, jnp.broadcast_to(b[...], (C, C)), 0.0), axis=1, keepdims=True),
                (C, LANES),
            )

    def place_taps():
        def blocks(places):
            row = lax.broadcasted_iota(jnp.int32, (C, 5 * C), 0)
            column = lax.broadcasted_iota(jnp.int32, (C, 5 * C), 1)
            hit = functools.reduce(jnp.logical_or, [column == row + p * C for p in places])
            return jnp.where(hit, 1.0, 0.0).astype(BF16)

        fifths = [blocks([0, 3]), blocks([1]), blocks([2, 4])]
        for i, w in enumerate((w2_ref, w1_ref)):
            for e in range(EDGES):
                for flip in range(2):
                    total = jnp.zeros((C, 5 * C), F32)
                    for m in range(3):
                        n = 2 - m if flip else m
                        tap = (w[0, n], w[2, n], w[n, 0], w[n, 2])[e]
                        total += lax.dot_general(
                            tap, fifths[m], (((0,), (0,)), ((), ())), preferred_element_type=F32
                        )
                    u_ref[i, 2 * e + flip] = total.astype(BF16)

    inputs[0].wait()
    to_rows(x_ref, xb, 1)

    def first_columns(f, carry):
        acc = jnp.zeros((C, LANES), F32)
        for r in range(rows):
            row = xb[f, r + 1].astype(F32)
            acc = keep(acc, r, row[:, :LANES], row[:, -LANES:])
        cp[f] = acc
        return carry

    lax.fori_loop(0, nf, first_columns, 0)
    d = lax.broadcasted_iota(jnp.int32, (1, LANES), 1)
    for p in range(half):
        seg = jnp.where(d % 2 == 1, p, last - p)
        target = jnp.where(d < 2 * rows, seg * rows + d // 2, -1)
        spread[:, p * LANES : (p + 1) * LANES] = one_hot(width, target)
    addrow[...] = jnp.zeros_like(addrow)
    pl.semaphore_wait(barrier, n_dev - 1)

    start_exchange(0, xb)
    for c in inputs[1:]:
        c.wait()
    place_weights()
    run_inner_products(0, xb)
    forward_exchange(0)
    place_sources()
    to_rows(og_ref, ogb, 0)
    pick(0)
    columns_forward(0, 0)
    run_inner(0, xb, finish_first)
    finish_ends(0, xb, None, True)
    columns_forward(0, 0)
    run_outer(0, xb, finish_first)

    start_exchange(1, hb)
    place_taps()
    run_inner_products(1, hb)
    forward_exchange(1)
    pick(1)
    columns_forward(1, 1)
    run_inner(1, hb, finish_second)
    finish_ends(1, hb, None, True)
    columns_forward(1, 1)
    run_outer(1, hb, finish_second)

    start_exchange(2, g2b)
    weight_products(0, g2b, hb, 1)
    start_sums(0)
    from_rows(rowsb, x_ref)
    out_copy = pltpu.make_async_copy(x_ref, out_hbm, s_out.at[nf])
    out_copy.start()
    run_inner_products(2, g2b)
    forward_exchange(2)
    pick(2)
    columns_backward(2, 0)
    run_inner(2, g2b, finish_third)
    finish_ends(2, g2b, 0, False)
    columns_backward(2, 0)
    run_outer(2, g2b, finish_third)

    start_exchange(3, g1b)
    weight_products(1, g1b, xb, 0)
    start_sums(1)
    add_sums(0)
    run_inner_products(3, g1b)
    forward_exchange(3)
    pick(3)
    columns_backward(3, 1)
    add_sums(1)
    run_inner(3, g1b, finish_last)
    finish_ends(3, g1b, 1, False)
    columns_backward(3, 1)
    run_outer(3, g1b, finish_last)

    gf_copies = [pltpu.make_async_copy(og_ref.at[f], gf_hbm.at[f], s_out.at[f]) for f in range(nf)]
    for f in range(nf):
        from_rows(rowsb, og_ref, [f])
        gf_copies[f].start()

    for i in range(2):
        for o in range(per):

            @pl.when(jnp.logical_not(is_owner(i, o)))
            def _():
                result_copy(i, o, me).wait_recv()
                sum_copy(i, o).wait_send()

            @pl.when(is_owner(i, o))
            def _():
                each_other(lambda j: result_copy(i, o, j).wait_send())

    out_copy.wait()
    for c in gf_copies:
        c.wait()
    for k, buf in enumerate((xb, hb, g2b, g1b)):
        for c in direct_copies(k):
            c.wait_send()
        for i, slot in enumerate(forward_slots()):
            forward_copy(k, i, slot).wait_send()
        ups = (halo_copies(k, buf)[0], ends_copies(k)[0], seg_copies(k)[0])
        downs = (halo_copies(k, buf)[1], ends_copies(k)[1], seg_copies(k)[1])

        @pl.when(jnp.logical_not(is_top))
        def _():
            for c in ups:
                c.wait_send()

        @pl.when(jnp.logical_not(is_bottom))
        def _():
            for c in downs:
                c.wait_send()

        @pl.when(is_top | is_bottom)
        def _():
            for j in range(tiles):
                same, across = ns_copies(k, j)
                across.wait_send()
                if j < last:
                    same.wait_send()


def results_kernel(out_ref, last_ref, sums_ref, out_dst, gf_dst, gw1, gb1, gw2, gb2):
    C = gw1.shape[-1]
    width = out_ref.shape[-1]
    out_dst[...] = out_ref[...]
    gf_dst[...] = last_ref[...]

    @pl.when(pl.program_id(0) == 0)
    def _():
        row = lax.broadcasted_iota(jnp.int32, (C, C), 0)
        column = lax.broadcasted_iota(jnp.int32, (C, C), 1)
        for i, (gw, gb) in enumerate(((gw2, gb2), (gw1, gb1))):
            for l in range(3):
                wide = sums_ref[i, l * C : (l + 1) * C] * (1.0 / width)
                for k in range(3):
                    gw[k, l] = pltpu.roll(wide, -k * C % (2 * LANES), 1)[:, :C]
                if l == 1:
                    at_first = pltpu.roll(wide, -3 * C % (2 * LANES), 1)[:, :1]
                    spread = jnp.where(row == column, jnp.broadcast_to(at_first, (C, C)), 0.0)
                    gb[...] = jnp.sum(spread, axis=0, keepdims=True)


def body(field_in, out_grad, weight_first, bias_first, weight_second, bias_second, face_links, corner_rules):
    faces_axis, tiles = lax.axis_size("face"), lax.axis_size("tile")
    nf, C, rows, width = field_in.shape
    n_dev = faces_axis * tiles
    taps_first = lambda w: jnp.transpose(w, (2, 3, 0, 1))
    slots = (nf + 1) // 2
    vm = pltpu.VMEM
    dma = pltpu.SemaphoreType.DMA
    padded = vm((nf, rows + 2, C, width), BF16)
    per = 3 * C // 8
    scratch = [
        vm(field_in.shape, BF16), vm(field_in.shape, BF16),
        vm((3, 3, C, C), BF16), vm((3, 3, C, C), BF16), vm((1, C), F32), vm((1, C), F32), dma((6,)), dma((nf + 1,)),
        vm((nf, rows, C, width), F32),
        vm((nf, 2 * LANES, LANES), BF16), vm((2, nf * LANES, LANES), BF16),
        vm((4, 3 * C, 3 * C), BF16),
        vm((2, 2 * EDGES, C, 5 * C), BF16),
        vm((2, C, LANES), F32),
        padded, padded, padded, padded,
        vm((nf, rows, C, width), BF16),
        vm((nf, rows, C, width), BF16),
        vm((nf, rows, C, width), F32),
        vm((nf, C, LANES), F32),
        *[vm((4 * faces_axis, slots, C, LANES), BF16)] * 4,
        vm((4, nf, C, LANES), BF16),
        vm((4, 2, nf, C, LANES), BF16),
        vm((4, nf, C, LANES), F32),
        vm((4, 2, C, LANES), BF16),
        vm((4, tiles, C, LANES), BF16),
        vm((nf, C, width), F32),
        vm((4, tiles // 2, slots, C, LANES), BF16),
        vm((width, tiles // 2 * LANES), BF16),
        vm((nf, C, LANES), F32),
        vm((2, nf, C, width), F32),
        vm((2, 3 * C, 2 * LANES), F32),
        vm((2, n_dev, 8, 2 * LANES), F32),
        dma((4, 2)), dma((4, 2)), dma((4, 4)), dma((4, 7)), dma((4, 2 * tiles)), dma((4, 4 * faces_axis)),
        dma((4, 2)), dma((4, 2)), dma((4, 2)), dma((4, tiles)),
        dma((2, per)), dma((2, n_dev)), dma((2, n_dev)), dma((2, per)),
    ]
    vmem = pl.BlockSpec(memory_space=pltpu.VMEM)
    smem = pl.BlockSpec(memory_space=pltpu.SMEM)
    hbm = pl.BlockSpec(memory_space=pltpu.HBM)
    flops = 2 * 6 * 9 * C * C * nf * rows * width
    natural, last_rows, sums = pl.pallas_call(
        functools.partial(fused_kernel, faces_axis, tiles),
        in_specs=[smem, smem] + [hbm] * 6,
        out_specs=[hbm, hbm, vmem],
        out_shape=[
            jax.ShapeDtypeStruct(field_in.shape, BF16),
            jax.ShapeDtypeStruct(field_in.shape, BF16),
            jax.ShapeDtypeStruct((2, 3 * C, 2 * LANES), F32),
        ],
        scratch_shapes=scratch,
        compiler_params=pltpu.CompilerParams(vmem_limit_bytes=57 << 20, collective_id=0, has_side_effects=True),
        cost_estimate=pl.CostEstimate(flops=flops, bytes_accessed=10**7, transcendentals=5 * 10**6),
    )(
        jnp.transpose(face_links, (2, 1, 0)), jnp.transpose(corner_rules), field_in, out_grad,
        taps_first(weight_first), taps_first(weight_second), bias_first[None], bias_second[None],
    )
    weight_shape = jax.ShapeDtypeStruct((3, 3, C, C), F32)
    bias_shape = jax.ShapeDtypeStruct((1, C), F32)
    face_spec = pl.BlockSpec((1, C, rows, width), lambda f: (f, 0, 0, 0))
    whole = lambda shape: pl.BlockSpec(shape, lambda f: (0,) * len(shape))
    output, grad_field, gw1, gb1, gw2, gb2 = pl.pallas_call(
        results_kernel,
        grid=(nf,),
        in_specs=[face_spec, face_spec, whole(sums.shape)],
        out_specs=[face_spec, face_spec] + [whole(a.shape) for a in (weight_shape, bias_shape) * 2],
        out_shape=[jax.ShapeDtypeStruct(field_in.shape, BF16)] * 2 + [weight_shape, bias_shape] * 2,
        compiler_params=pltpu.CompilerParams(vmem_limit_bytes=57 << 20),
    )(natural, last_rows, sums)
    back = lambda g: jnp.transpose(g, (2, 3, 0, 1))
    return output, grad_field, back(gw1), gb1[0], back(gw2), gb2[0]


def solution(mesh):
    cells = P("face", None, "tile", None)
    return jax.shard_map(
        body,
        mesh=mesh,
        in_specs=(cells, cells, P(), P(), P(), P(), P(), P()),
        out_specs=(cells, cells, P(), P(), P(), P()),
        check_vma=False,
    )
```

```python
import functools

import jax
import jax.numpy as jnp
from jax import lax
from jax.experimental import pallas as pl
from jax.experimental.pallas import tpu as pltpu
from jax.sharding import PartitionSpec as P

INV_ROOT_TWO = 0.7071067811865476
INV_ROOT_TWO_PI = 0.3989422804014327
F32 = jnp.float32
BF16 = jnp.bfloat16
LANES = 128
MESH_ID = pl.DeviceIdType.MESH
EDGES = 4
GROUP = 16


def gelu_pair(values):
    normal_cdf = 0.5 * (1.0 + lax.erf(values * INV_ROOT_TWO))
    normal_pdf = jnp.exp(-0.5 * values * values) * INV_ROOT_TWO_PI
    return (values * normal_cdf, normal_cdf + values * normal_pdf)


def one_hot(rows, target):
    row = lax.broadcasted_iota(jnp.int32, (rows, target.shape[1]), 0)
    return jnp.where(row == target, 1.0, 0.0).astype(BF16)


def turn(a, shift):
    return pltpu.roll(a, shift % LANES, 1)


def from_rows(src, dst, only=None):
    nf, rows, C, _ = src.shape
    for f in range(nf) if only is None else only:
        for r0 in range(0, rows, GROUP):
            n = min(GROUP, rows - r0)
            for c0 in range(0, C, GROUP):
                block = src[f, r0 : r0 + n, c0 : c0 + GROUP]
                if n < GROUP:
                    block = jnp.swapaxes(block.astype(F32), 0, 1).astype(BF16)
                else:
                    block = jnp.swapaxes(block, 0, 1)
                dst[f, c0 : c0 + GROUP, r0 : r0 + n] = block


def fused_kernel(
    faces_axis, tiles, links, rules, x_hbm, og_hbm, w1_hbm, w2_hbm, b1_hbm, b2_hbm,
    out_hbm, gf_hbm, gw_ref,
    x_ref, og_ref, w1_ref, w2_ref, b1_ref, b2_ref, s_in, s_out, pre_ref, we_place, ns_place,
    wst_ref, u_ref, b_ref,
    xb, hb, g2b, g1b, ogb, rowsb, slope_ref, cp, packs0, packs1, packs2, packs3, gp, gpn, full, seg_out, seg_in, line_in, ns_out, spread,
    addcol, addrow, part, landed,
    s_halo, r_halo, s_direct, s_fwd, s_ns, r_packs, s_ends, r_ends, s_seg, r_seg, s_sum, r_sum, s_res, r_res,
):
    nf, C, rows, width = x_ref.shape
    packs = (packs0, packs1, packs2, packs3)
    slots = packs0.shape[1]
    n_dev = faces_axis * tiles
    face = lax.axis_index("face")
    tile = lax.axis_index("tile")
    me = face * tiles + tile
    last = tiles - 1
    mirror_tile = last - tile
    half = tiles // 2
    lane = lax.broadcasted_iota(jnp.int32, (C, LANES), 1)
    even = lane % 2 == 0
    is_top = tile == 0
    is_bottom = tile == last
    top_f = jnp.where(is_top, 1.0, 0.0)
    bottom_f = jnp.where(is_bottom, 1.0, 0.0)
    upper_half = jnp.where(tile >= half, 1, 0)
    peer = lax.rem(face + 2, faces_axis)
    sibling = face + 1 - 2 * lax.rem(face, 2)
    sibling_peer = lax.rem(sibling + 2, faces_axis)

    def at(j):
        return (lax.div(j, tiles), lax.rem(j, tiles))

    def each_other(body):
        def step(j, carry):
            @pl.when(j != me)
            def _():
                body(j)

            return carry

        lax.fori_loop(0, n_dev, step, 0)

    barrier = pltpu.get_barrier_semaphore()
    each_other(lambda j: pl.semaphore_signal(barrier, inc=1, device_id=at(j), device_id_type=MESH_ID))

    inputs = [
        pltpu.make_async_copy(src, dst, s_in.at[i])
        for i, (src, dst) in enumerate(
            (
                (x_hbm, x_ref), (w1_hbm, w1_ref), (w2_hbm, w2_ref), (b1_hbm, b1_ref), (b2_hbm, b2_ref),
                (og_hbm, og_ref),
            )
        )
    ]
    for c in inputs:
        c.start()

    def to_rows(src, dst, first):
        for f in range(nf):
            for r0 in range(0, rows, GROUP):
                n = min(GROUP, rows - r0)
                for c0 in range(0, C, GROUP):
                    block = src[f, c0 : c0 + GROUP, r0 : r0 + n]
                    if n < GROUP:
                        block = jnp.swapaxes(block.astype(F32), 0, 1).astype(BF16)
                    else:
                        block = jnp.swapaxes(block, 0, 1)
                    dst[f, first + r0 : first + r0 + n, c0 : c0 + GROUP] = block

    def keep(acc, r, lo, hi):
        mixed = turn(jnp.where(lane == LANES - 1, hi, lo), 2 * r)
        return jnp.where((lane == 2 * r) | (lane == (2 * r - 1) % LANES), mixed, acc)

    def copy(src, dst, send, recv, device):
        return pltpu.make_async_remote_copy(src, dst, send, recv, device, MESH_ID)

    ns_base = 2 * faces_axis

    def halo_copies(k, buf):
        up = copy(buf.at[:, 1], buf.at[:, rows + 1], s_halo.at[k, 0], r_halo.at[k, 1], (face, tile - 1))
        down = copy(buf.at[:, rows], buf.at[:, 0], s_halo.at[k, 1], r_halo.at[k, 0], (face, tile + 1))
        return up, down

    def direct_copies(k):
        own = packs[k].at[face]
        here = face
        there = faces_axis + face
        return [
            copy(own, packs[k].at[there], s_direct.at[k, 0], r_packs.at[k, there], (face, mirror_tile)),
            copy(own, packs[k].at[there], s_direct.at[k, 1], r_packs.at[k, there], (peer, mirror_tile)),
            copy(own, packs[k].at[here], s_direct.at[k, 2], r_packs.at[k, here], (peer, tile)),
            copy(own, packs[k].at[here], s_direct.at[k, 3], r_packs.at[k, here], (sibling, tile)),
        ]

    def ns_slot():
        return ns_base + jnp.where(is_top, 0, 1) * faces_axis + face

    def ns_copies(k, j):
        t = jnp.where(is_top, last - j, j)
        src = ns_out.at[k, min(j, last - j)]
        slot = ns_slot()
        return [
            copy(src, packs[k].at[slot], s_ns.at[k, j], r_packs.at[k, slot], (face, t)),
            copy(src, packs[k].at[slot], s_ns.at[k, tiles + j], r_packs.at[k, slot], (peer, t)),
        ]

    def forward_slots():
        return [faces_axis + face, peer, faces_axis + peer] + [
            ns_base + n * faces_axis + q for n in range(2) for q in (face, peer)
        ]

    def arriving_slots():
        return [sibling, faces_axis + sibling, sibling_peer, faces_axis + sibling_peer] + [
            ns_base + n * faces_axis + q for n in range(2) for q in (sibling, sibling_peer)
        ]

    def forward_copy(k, i, slot):
        ref = packs[k].at[slot]
        return copy(ref, ref, s_fwd.at[k, i], r_packs.at[k, slot], (sibling, tile))

    def ends_copies(k):
        return (
            copy(gp.at[k], gpn.at[k, 1], s_ends.at[k, 0], r_ends.at[k, 1], (face, tile - 1)),
            copy(gp.at[k], gpn.at[k, 0], s_ends.at[k, 1], r_ends.at[k, 0], (face, tile + 1)),
        )

    def seg_copies(k):
        dst = seg_in.at[k, tile]
        return (
            copy(seg_out.at[k, 0], dst, s_seg.at[k, 0], r_seg.at[k, tile], (face, 0)),
            copy(seg_out.at[k, 1], dst, s_seg.at[k, 1], r_seg.at[k, tile], (face, last)),
        )

    def start_exchange(k, buf):
        for slot in range(slots):
            faces_here = [f for f in range(nf) if f // 2 == slot]
            packed = turn(cp[faces_here[0]], 1)
            if len(faces_here) > 1:
                packed = jnp.where(lane < 64, packed, turn(cp[faces_here[1]], 65))
            packs[k][face, slot] = packed.astype(BF16)
        for c in direct_copies(k):
            c.start()

        @pl.when(is_top | is_bottom)
        def _():
            lines = jnp.concatenate(
                [jnp.where(is_top, buf[f, 1].astype(F32), buf[f, rows].astype(F32)) for f in range(nf)], axis=0
            ).astype(BF16)
            spreads = jnp.dot(lines, spread[...], preferred_element_type=F32)
            for p in range(half):
                part_p = spreads[:, p * LANES : (p + 1) * LANES]
                for slot in range(slots):
                    faces_here = [f for f in range(nf) if f // 2 == slot]
                    first = faces_here[0]
                    packed = part_p[first * C : (first + 1) * C]
                    if len(faces_here) > 1:
                        packed = jnp.where(lane < 64, packed, turn(part_p[(first + 1) * C : (first + 2) * C], 64))
                    ns_out[k, p, slot] = packed.astype(BF16)
            packs[k][ns_slot()] = ns_out[k, 0]
            for j in range(tiles):
                same, across = ns_copies(k, j)
                across.start()
                if j < last:
                    same.start()

        up, down = halo_copies(k, buf)

        @pl.when(jnp.logical_not(is_top))
        def _():
            up.start()

        @pl.when(jnp.logical_not(is_bottom))
        def _():
            down.start()

    def not_own_ns(i):
        n, which = divmod(i - 3, 2)
        if which:
            return jnp.bool_(True)
        return jnp.logical_not(is_top if n == 0 else is_bottom)

    def forward_exchange(k):
        for i, slot in enumerate(forward_slots()):
            fwd = forward_copy(k, i, slot)
            if i < 3:
                fwd.wait_recv()
            else:

                @pl.when(not_own_ns(i))
                def _():
                    fwd.wait_recv()

            fwd.start()

    def link(f, e):
        return links[0, e, face * nf + f], links[1, e, face * nf + f], links[2, e, face * nf + f]

    def source(f, e):
        g, e2, flip = link(f, e)
        q2, f2 = lax.div(g, nf), lax.rem(g, nf)
        we = lax.div(e2, 2)
        idx = we * (flip * faces_axis + q2) + (1 - we) * (ns_base + e2 * faces_axis + q2)
        return idx, lax.div(f2, 2)

    def source_lanes(f, e):
        g, e2, flip = link(f, e)
        we = lax.div(e2, 2)
        other = upper_half + flip - 2 * upper_half * flip
        bit = we * (3 - e2) + (1 - we) * (1 - other)
        return 64 * lax.rem(lax.rem(g, nf), 2) + bit + flip * 2 * (rows - 1), 2 - 4 * flip

    def place_sources():
        d = lax.broadcasted_iota(jnp.int32, (1, LANES), 1)
        west_r = d // 2
        west_ok = (d % 2 == 0) & (d < 2 * rows)
        east_r = ((d + 1) % LANES) // 2
        east_ok = (d % 2 == 1) & (east_r < rows)
        for f in range(nf):
            for j, (e, ok, r) in enumerate(((2, west_ok, west_r), (3, east_ok, east_r))):
                start, step = source_lanes(f, e)
                we_place[f, j * LANES : (j + 1) * LANES] = one_hot(LANES, jnp.where(ok, start + step * r, -1))
            ok = (d >= f * rows) & (d < (f + 1) * rows)
            for e in range(2):
                start, step = source_lanes(f, e)
                ns_place[e, f * LANES : (f + 1) * LANES] = one_hot(
                    LANES, jnp.where(ok, start + step * (d - f * rows), -1)
                )

    def pick(k):
        for slot in arriving_slots():
            copy(packs[k].at[slot], packs[k].at[slot], s_fwd.at[k, 0], r_packs.at[k, slot], (sibling, tile)).wait_recv()

        def taken(f, e):
            idx, slot = source(f, e)
            return packs[k][idx, slot]

        for e in range(2):
            srcs = jnp.concatenate([taken(f, e) for f in range(nf)], axis=1)
            seg_out[k, e] = jnp.dot(srcs, ns_place[e], preferred_element_type=F32).astype(BF16)
        for f in range(nf):
            srcs = jnp.concatenate([taken(f, 2), taken(f, 3)], axis=1)
            gp[k, f] = jnp.dot(srcs, we_place[f], preferred_element_type=F32).astype(BF16)
        up, down = ends_copies(k)
        to_top, to_bottom = seg_copies(k)

        @pl.when(is_top)
        def _():
            seg_in[k, 0] = seg_out[k, 0]

        @pl.when(is_bottom)
        def _():
            seg_in[k, last] = seg_out[k, 1]

        @pl.when(jnp.logical_not(is_top))
        def _():
            to_top.start()
            up.start()

        @pl.when(jnp.logical_not(is_bottom))
        def _():
            to_bottom.start()
            down.start()

        for f in range(nf):
            full[k, f] = gp[k, f].astype(F32)

    def stack3(a, first):
        return [turn(a, first), a, turn(a, -first)]

    def columns_forward(k, which):
        w = wst_ref[which]
        for f in range(nf):
            stacked = jnp.concatenate(stack3(full[k, f], 2), axis=0).astype(BF16)
            y = jnp.dot(w, stacked, preferred_element_type=F32)
            addcol[f] = jnp.where(even, y[:C], y[2 * C :])

    def end_rules(f, e):
        g, e2, flip = link(f, e)
        we = lax.div(e2, 2)
        first = rules[we * (e2 - 2) + (1 - we) * 2 * e2, g]
        final = rules[we * e2 + (1 - we) * (1 + 2 * e2), g]
        first = jnp.where(first == we, 1.0, 0.0)
        final = jnp.where(final == we, 1.0, 0.0)
        low = jnp.where(flip == 0, first, final)
        high = jnp.where(flip == 0, final, first)
        return e2 * 2 + flip, low, high

    def columns_backward(k, which):
        for f in range(nf):
            wu, wlow, whigh = end_rules(f, 2)
            eu, elow, ehigh = end_rules(f, 3)
            a = full[k, f]
            low = jnp.where(lane == 0, wlow, jnp.where(lane == LANES - 1, elow, 0.0)) * top_f
            high = jnp.where(lane == 2 * rows - 2, whigh, jnp.where(lane == 2 * rows - 3, ehigh, 0.0)) * bottom_f
            stacked = jnp.concatenate(stack3(a, -2) + [a * low, a * high], axis=0).astype(BF16)
            weights = jnp.concatenate([u_ref[which, wu], u_ref[which, eu]], axis=0)
            y = jnp.dot(weights, stacked, preferred_element_type=F32)
            addcol[f] = jnp.where(even, y[:C], y[C:]).astype(BF16).astype(F32)

    def finish_ends(k, buf, which, forward):
        above = (lane == LANES - 2) | (lane == LANES - 3)
        below = (lane == 2 * rows) | (lane == 2 * rows - 1)

        @pl.when(jnp.logical_not(is_top))
        def _():
            copy(gpn.at[k, 0], gpn.at[k, 0], s_ends.at[k, 0], r_ends.at[k, 0], (face, tile - 1)).wait_recv()
            copy(buf.at[:, 0], buf.at[:, 0], s_halo.at[k, 0], r_halo.at[k, 0], (face, tile - 1)).wait_recv()
            for f in range(nf):
                full[k, f] = jnp.where(above, turn(gpn[k, 0, f].astype(F32), -2 * rows), full[k, f])

        @pl.when(jnp.logical_not(is_bottom))
        def _():
            copy(gpn.at[k, 1], gpn.at[k, 1], s_ends.at[k, 1], r_ends.at[k, 1], (face, tile + 1)).wait_recv()
            hup_ref = buf.at[:, rows + 1]
            copy(hup_ref, hup_ref, s_halo.at[k, 1], r_halo.at[k, 1], (face, tile + 1)).wait_recv()
            for f in range(nf):
                full[k, f] = jnp.where(below, turn(gpn[k, 1, f].astype(F32), 2 * rows), full[k, f])

        def assemble(e):
            for t in range(tiles):

                @pl.when(tile != t)
                def _():
                    ref = seg_in.at[k, t]
                    copy(ref, ref, s_seg.at[k, 0], r_seg.at[k, t], (face, last - tile)).wait_recv()

            for f in range(nf):
                for i in range(width // LANES):
                    piece = jnp.zeros((C, LANES), F32)
                    for t in range(tiles):
                        if t * rows // LANES == i:
                            off = t * rows % LANES
                            moved = turn(seg_in[k, t].astype(F32), off - f * rows)
                            piece = jnp.where((lane >= off) & (lane < off + rows), moved, piece)
                    line_in[f, :, i * LANES : (i + 1) * LANES] = piece

            if forward:
                row = 0 if e == 0 else rows + 1
                for f in range(nf):
                    line = line_in[f]
                    buf[f, row] = line.astype(BF16)
                    ghost = full[k, f]
                    mixed = jnp.where(lane == LANES - 1, line[:, -LANES:], line[:, :LANES])
                    by_line_w = rules[2 * e, face * nf + f] == 0
                    by_line_e = rules[2 * e + 1, face * nf + f] == 0
                    if e == 0:
                        from_line, from_col = turn(mixed, -2), turn(ghost, -2)
                        at_w, at_e = LANES - 2, LANES - 3
                    else:
                        from_line, from_col = turn(mixed, 2 * rows), turn(ghost, 2)
                        at_w, at_e = 2 * rows, 2 * rows - 1
                    corner_w = jnp.where(by_line_w, from_line, from_col)
                    corner_e = jnp.where(by_line_e, from_line, from_col)
                    full[k, f] = jnp.where(lane == at_w, corner_w, jnp.where(lane == at_e, corner_e, ghost))
            else:
                row = 0 if e == 0 else rows + 1
                wide = lax.broadcasted_iota(jnp.int32, (C, width), 1)
                for f in range(nf):
                    buf[f, row] = jnp.zeros((C, width), BF16)
                    u, low, high = end_rules(f, e)
                    line = line_in[f]
                    ahead = jnp.where(wide == width - 1, 0.0, pltpu.roll(line, width - 1, 1))
                    behind = jnp.where(wide == 0, 0.0, pltpu.roll(line, 1, 1))
                    ends = [
                        line * jnp.where(wide == 0, low, 0.0), line * jnp.where(wide == width - 1, high, 0.0)
                    ]
                    stacked = jnp.concatenate([ahead, line, behind] + ends, axis=0).astype(BF16)
                    y = jnp.dot(u_ref[which, u], stacked, preferred_element_type=F32)
                    addrow[e, f] = y.astype(BF16).astype(F32)

        @pl.when(is_top)
        def _():
            assemble(0)

        @pl.when(is_bottom)
        def _():
            assemble(1)

    def cut(a, i):
        return a[:, i * LANES : (i + 1) * LANES]

    def conv_row(w, buf, f, r, ins):
        y = jnp.dot(w, buf[f, pl.ds(r, 3)].reshape(3 * C, width), preferred_element_type=F32)
        first, final = lane == 0, lane == LANES - 1
        parts = width // LANES
        west = [turn(cut(y[:C], i), 1) for i in range(parts)]
        east = [turn(cut(y[2 * C :], i), -1) for i in range(parts)]
        out = []
        for i in range(parts):
            left = jnp.where(first, west[i - 1] if i > 0 else ins, west[i])
            right = jnp.where(final, east[i + 1] if i < parts - 1 else ins, east[i])
            out.append(cut(y[C : 2 * C], i) + left + right)
        return out

    def run_inner_products(which, buf):
        def face_step(f, carry):
            w = wst_ref[which]
            zero = jnp.zeros((C, LANES), F32)
            for r in range(1, rows - 1):
                for i, p in enumerate(conv_row(w, buf, f, r, zero)):
                    pre_ref[f, r, :, i * LANES : (i + 1) * LANES] = p
            return carry

        lax.fori_loop(0, nf, face_step, 0)

    def with_columns(f, r, ghost):
        ins = turn(ghost, -2 * r)
        total = [cut(pre_ref[f, r], i) for i in range(width // LANES)]
        total[0] = total[0] + jnp.where(lane == 0, ins, 0.0)
        total[-1] = total[-1] + jnp.where(lane == LANES - 1, ins, 0.0)
        return total

    def do_rows(which, buf, f, rs, finish, acc):
        ghost = addcol[f]
        for r in rs:
            if r in (0, rows - 1):
                total = conv_row(wst_ref[which], buf, f, r, turn(ghost, -2 * r))
            else:
                total = with_columns(f, r, ghost)
            kept = finish(f, r, total)
            if kept is not None:
                acc = keep(acc, r, kept[0], kept[-1])
        return acc

    def run_inner(which, buf, finish):
        def face_step(f, carry):
            cp[f] = do_rows(which, buf, f, range(1, rows - 1), finish, jnp.zeros((C, LANES), F32))
            return carry

        lax.fori_loop(0, nf, face_step, 0)

    def run_outer(which, buf, finish):
        accs = [do_rows(which, buf, f, (0, rows - 1), finish, cp[f]) for f in range(nf)]
        for f in range(nf):
            cp[f] = accs[f]

    def put(ref, f, r, parts, dtype):
        ref[f, r] = jnp.concatenate([p.astype(dtype) for p in parts], axis=1)

    def bias(i):
        return jnp.broadcast_to(b_ref[i], (C, LANES))

    def finish_first(f, r, total):
        pairs = [gelu_pair(p + bias(0)) for p in total]
        values = [p[0] for p in pairs]
        put(slope_ref, f, r, [p[1] for p in pairs], F32)
        put(hb, f, r + 1, values, BF16)
        return values

    def finish_second(f, r, total):
        pairs = [gelu_pair(p + bias(1)) for p in total]
        put(rowsb, f, r, [p[0] for p in pairs], BF16)
        og = ogb[f, r].astype(F32)
        grads = [og[:, i * LANES : (i + 1) * LANES] * p[1] for i, p in enumerate(pairs)]
        put(g2b, f, r + 1, grads, BF16)
        return grads

    def with_row(f, r, total):
        if r not in (0, rows - 1):
            return total
        e = 0 if r == 0 else 1
        return [p + addrow[e, f, :, i * LANES : (i + 1) * LANES] for i, p in enumerate(total)]

    def finish_third(f, r, total):
        total = with_row(f, r, total)
        slope = slope_ref[f, r]
        grads = [p * slope[:, i * LANES : (i + 1) * LANES] for i, p in enumerate(total)]
        put(g1b, f, r + 1, grads, BF16)
        return grads

    def finish_last(f, r, total):
        put(rowsb, f, r, with_row(f, r, total), BF16)
        return None

    def weight_products(i, grad_buf, field_buf, k):
        part[i] = jnp.zeros_like(part[i])
        ones = jnp.ones((16, width), BF16)

        def face_step(f, carry):
            first, final = lane == 0, lane == LANES - 1
            zero = jnp.zeros((C, LANES), F32)
            lefts, rights = [], []
            for r in range(rows):
                grad = grad_buf[f, r + 1]
                wide = grad.astype(F32)
                cuts = [wide[:, j : j + LANES] for j in range(0, width, LANES)]
                ahead = [turn(a, -1) for a in cuts]
                behind = [turn(a, 1) for a in cuts]
                n = len(cuts)
                shift_a = [jnp.where(final, ahead[j + 1] if j < n - 1 else zero, ahead[j]) for j in range(n)]
                shift_b = [jnp.where(first, behind[j - 1] if j > 0 else zero, behind[j]) for j in range(n)]
                lefts.append(
                    jnp.concatenate(
                        [
                            jnp.concatenate([a.astype(BF16) for a in shift_a], axis=1),
                            grad,
                            jnp.concatenate([b.astype(BF16) for b in shift_b], axis=1),
                        ],
                        axis=0,
                    )
                )
                rights.append(
                    jnp.concatenate([field_buf[f, pl.ds(r, 3)].reshape(3 * C, width), ones], axis=0)
                )
            inside = (lane < 2 * rows - 1) | (lane == LANES - 1)
            edge = jnp.where(inside, cp[f], 0.0)
            lefts.append(
                jnp.concatenate([jnp.where(even, edge, 0.0), zero, jnp.where(even, 0.0, edge)], axis=0).astype(BF16)
            )
            rights.append(
                jnp.concatenate(stack3(full[k, f], 2) + [jnp.zeros((16, LANES), F32)], axis=0).astype(BF16)
            )
            products = lax.dot_general(
                jnp.concatenate(lefts, axis=1),
                jnp.concatenate(rights, axis=1),
                (((1,), (1,)), ((), ())),
                preferred_element_type=F32,
            )
            part[i, :, : 3 * C + 16] += products
            return carry

        lax.fori_loop(0, nf, face_step, 0)

    block = 8
    per = 3 * C // block
    middle = max(tiles - 2, 1)

    def owner(i, o):
        j = o + 6 * i
        return (j // middle % faces_axis, 1 + j % middle)

    def is_owner(i, o):
        f, t = owner(i, o)
        return (face == f) & (tile == t)

    def block_of(ref, i, o):
        return ref.at[i, pl.ds(o * block, block)]

    def sum_copy(i, o):
        return copy(block_of(part, i, o), landed.at[i, me], s_sum.at[i, o], r_sum.at[i, me], owner(i, o))

    def start_sums(i):
        for o in range(per):
            c = sum_copy(i, o)

            @pl.when(jnp.logical_not(is_owner(i, o)))
            def _():
                c.start()

    def result_copy(i, o, j):
        ref = block_of(gw_ref, i, o)
        return copy(ref, ref, s_res.at[i, j], r_res.at[i, o], at(j))

    def add_sums(i):
        for o in range(per):

            @pl.when(is_owner(i, o))
            def _():
                each_other(
                    lambda j: copy(
                        landed.at[i, j], landed.at[i, j], s_sum.at[i, 0], r_sum.at[i, j], at(j)
                    ).wait_recv()
                )
                landed[i, me] = block_of(part, i, o)[...]
                total = lax.fori_loop(1, n_dev, lambda j, t: t + landed[i, j], landed[i, 0])
                block_of(gw_ref, i, o)[...] = total
                each_other(lambda j: result_copy(i, o, j).start())

    def place_weights():
        def blocks(count, places):
            row = lax.broadcasted_iota(jnp.int32, (C, count * C), 0)
            column = lax.broadcasted_iota(jnp.int32, (C, count * C), 1)
            hit = functools.reduce(jnp.logical_or, [column == row + p * C for p in places])
            return jnp.where(hit, 1.0, 0.0).astype(BF16)

        thirds = [blocks(3, [k]) for k in range(3)]
        straight = lambda a, e: jnp.dot(a, e, preferred_element_type=F32)
        turned = lambda a, e: lax.dot_general(a, e, (((0,), (0,)), ((), ())), preferred_element_type=F32)
        for which, w in ((0, w1_ref), (1, w2_ref)):
            for l in range(3):
                total = sum(straight(w[k, l], thirds[k]) for k in range(3))
                wst_ref[which, l * C : (l + 1) * C] = total.astype(BF16)
        for which, w in ((2, w2_ref), (3, w1_ref)):
            for l in range(3):
                total = sum(turned(w[2 - k, 2 - l], thirds[k]) for k in range(3))
                wst_ref[which, l * C : (l + 1) * C] = total.astype(BF16)
        row = lax.broadcasted_iota(jnp.int32, (C, C), 0)
        column = lax.broadcasted_iota(jnp.int32, (C, C), 1)
        for i, b in enumerate((b1_ref, b2_ref)):
            b_ref[i] = jnp.broadcast_to(
                jnp.sum(jnp.where(row == column, jnp.broadcast_to(b[...], (C, C)), 0.0), axis=1, keepdims=True),
                (C, LANES),
            )

    def place_taps():
        def blocks(places):
            row = lax.broadcasted_iota(jnp.int32, (C, 5 * C), 0)
            column = lax.broadcasted_iota(jnp.int32, (C, 5 * C), 1)
            hit = functools.reduce(jnp.logical_or, [column == row + p * C for p in places])
            return jnp.where(hit, 1.0, 0.0).astype(BF16)

        fifths = [blocks([0, 3]), blocks([1]), blocks([2, 4])]
        for i, w in enumerate((w2_ref, w1_ref)):
            for e in range(EDGES):
                for flip in range(2):
                    total = jnp.zeros((C, 5 * C), F32)
                    for m in range(3):
                        n = 2 - m if flip else m
                        tap = (w[0, n], w[2, n], w[n, 0], w[n, 2])[e]
                        total += lax.dot_general(
                            tap, fifths[m], (((0,), (0,)), ((), ())), preferred_element_type=F32
                        )
                    u_ref[i, 2 * e + flip] = total.astype(BF16)

    inputs[0].wait()
    to_rows(x_ref, xb, 1)

    def first_columns(f, carry):
        acc = jnp.zeros((C, LANES), F32)
        for r in range(rows):
            row = xb[f, r + 1].astype(F32)
            acc = keep(acc, r, row[:, :LANES], row[:, -LANES:])
        cp[f] = acc
        return carry

    lax.fori_loop(0, nf, first_columns, 0)
    d = lax.broadcasted_iota(jnp.int32, (1, LANES), 1)
    for p in range(half):
        seg = jnp.where(d % 2 == 1, p, last - p)
        target = jnp.where(d < 2 * rows, seg * rows + d // 2, -1)
        spread[:, p * LANES : (p + 1) * LANES] = one_hot(width, target)
    addrow[...] = jnp.zeros_like(addrow)
    pl.semaphore_wait(barrier, n_dev - 1)

    start_exchange(0, xb)
    for c in inputs[1:]:
        c.wait()
    place_weights()
    run_inner_products(0, xb)
    forward_exchange(0)
    place_sources()
    to_rows(og_ref, ogb, 0)
    pick(0)
    columns_forward(0, 0)
    run_inner(0, xb, finish_first)
    finish_ends(0, xb, None, True)
    columns_forward(0, 0)
    run_outer(0, xb, finish_first)

    start_exchange(1, hb)
    place_taps()
    run_inner_products(1, hb)
    forward_exchange(1)
    pick(1)
    columns_forward(1, 1)
    run_inner(1, hb, finish_second)
    finish_ends(1, hb, None, True)
    columns_forward(1, 1)
    run_outer(1, hb, finish_second)

    start_exchange(2, g2b)
    weight_products(0, g2b, hb, 1)
    start_sums(0)
    from_rows(rowsb, x_ref)
    out_copy = pltpu.make_async_copy(x_ref, out_hbm, s_out.at[nf])
    out_copy.start()
    run_inner_products(2, g2b)
    forward_exchange(2)
    pick(2)
    columns_backward(2, 0)
    run_inner(2, g2b, finish_third)
    finish_ends(2, g2b, 0, False)
    columns_backward(2, 0)
    run_outer(2, g2b, finish_third)

    start_exchange(3, g1b)
    weight_products(1, g1b, xb, 0)
    start_sums(1)
    add_sums(0)
    run_inner_products(3, g1b)
    forward_exchange(3)
    pick(3)
    columns_backward(3, 1)
    add_sums(1)
    run_inner(3, g1b, finish_last)
    finish_ends(3, g1b, 1, False)
    columns_backward(3, 1)
    run_outer(3, g1b, finish_last)

    gf_copies = [pltpu.make_async_copy(og_ref.at[f], gf_hbm.at[f], s_out.at[f]) for f in range(nf)]
    for f in range(nf):
        from_rows(rowsb, og_ref, [f])
        gf_copies[f].start()

    for i in range(2):
        for o in range(per):

            @pl.when(jnp.logical_not(is_owner(i, o)))
            def _():
                result_copy(i, o, me).wait_recv()
                sum_copy(i, o).wait_send()

            @pl.when(is_owner(i, o))
            def _():
                each_other(lambda j: result_copy(i, o, j).wait_send())

    out_copy.wait()
    for c in gf_copies:
        c.wait()
    for k, buf in enumerate((xb, hb, g2b, g1b)):
        for c in direct_copies(k):
            c.wait_send()
        for i, slot in enumerate(forward_slots()):
            forward_copy(k, i, slot).wait_send()
        ups = (halo_copies(k, buf)[0], ends_copies(k)[0], seg_copies(k)[0])
        downs = (halo_copies(k, buf)[1], ends_copies(k)[1], seg_copies(k)[1])

        @pl.when(jnp.logical_not(is_top))
        def _():
            for c in ups:
                c.wait_send()

        @pl.when(jnp.logical_not(is_bottom))
        def _():
            for c in downs:
                c.wait_send()

        @pl.when(is_top | is_bottom)
        def _():
            for j in range(tiles):
                same, across = ns_copies(k, j)
                across.wait_send()
                if j < last:
                    same.wait_send()


def results_kernel(out_ref, last_ref, sums_ref, out_dst, gf_dst, gw1, gb1, gw2, gb2):
    C = gw1.shape[-1]
    width = out_ref.shape[-1]
    out_dst[...] = out_ref[...]
    gf_dst[...] = last_ref[...]

    @pl.when(pl.program_id(0) == 0)
    def _():
        row = lax.broadcasted_iota(jnp.int32, (C, C), 0)
        column = lax.broadcasted_iota(jnp.int32, (C, C), 1)
        for i, (gw, gb) in enumerate(((gw2, gb2), (gw1, gb1))):
            for l in range(3):
                wide = sums_ref[i, l * C : (l + 1) * C] * (1.0 / width)
                for k in range(3):
                    gw[k, l] = pltpu.roll(wide, -k * C % (2 * LANES), 1)[:, :C]
                if l == 1:
                    at_first = pltpu.roll(wide, -3 * C % (2 * LANES), 1)[:, :1]
                    spread = jnp.where(row == column, jnp.broadcast_to(at_first, (C, C)), 0.0)
                    gb[...] = jnp.sum(spread, axis=0, keepdims=True)


def body(field_in, out_grad, weight_first, bias_first, weight_second, bias_second, face_links, corner_rules):
    faces_axis, tiles = lax.axis_size("face"), lax.axis_size("tile")
    nf, C, rows, width = field_in.shape
    n_dev = faces_axis * tiles
    taps_first = lambda w: jnp.transpose(w, (2, 3, 0, 1))
    slots = (nf + 1) // 2
    vm = pltpu.VMEM
    dma = pltpu.SemaphoreType.DMA
    padded = vm((nf, rows + 2, C, width), BF16)
    per = 3 * C // 8
    scratch = [
        vm(field_in.shape, BF16), vm(field_in.shape, BF16),
        vm((3, 3, C, C), BF16), vm((3, 3, C, C), BF16), vm((1, C), F32), vm((1, C), F32), dma((6,)), dma((nf + 1,)),
        vm((nf, rows, C, width), F32),
        vm((nf, 2 * LANES, LANES), BF16), vm((2, nf * LANES, LANES), BF16),
        vm((4, 3 * C, 3 * C), BF16),
        vm((2, 2 * EDGES, C, 5 * C), BF16),
        vm((2, C, LANES), F32),
        padded, padded, padded, padded,
        vm((nf, rows, C, width), BF16),
        vm((nf, rows, C, width), BF16),
        vm((nf, rows, C, width), F32),
        vm((nf, C, LANES), F32),
        *[vm((4 * faces_axis, slots, C, LANES), BF16)] * 4,
        vm((4, nf, C, LANES), BF16),
        vm((4, 2, nf, C, LANES), BF16),
        vm((4, nf, C, LANES), F32),
        vm((4, 2, C, LANES), BF16),
        vm((4, tiles, C, LANES), BF16),
        vm((nf, C, width), F32),
        vm((4, tiles // 2, slots, C, LANES), BF16),
        vm((width, tiles // 2 * LANES), BF16),
        vm((nf, C, LANES), F32),
        vm((2, nf, C, width), F32),
        vm((2, 3 * C, 2 * LANES), F32),
        vm((2, n_dev, 8, 2 * LANES), F32),
        dma((4, 2)), dma((4, 2)), dma((4, 4)), dma((4, 7)), dma((4, 2 * tiles)), dma((4, 4 * faces_axis)),
        dma((4, 2)), dma((4, 2)), dma((4, 2)), dma((4, tiles)),
        dma((2, per)), dma((2, n_dev)), dma((2, n_dev)), dma((2, per)),
    ]
    vmem = pl.BlockSpec(memory_space=pltpu.VMEM)
    smem = pl.BlockSpec(memory_space=pltpu.SMEM)
    hbm = pl.BlockSpec(memory_space=pltpu.HBM)
    flops = 2 * 6 * 9 * C * C * nf * rows * width
    natural, last_rows, sums = pl.pallas_call(
        functools.partial(fused_kernel, faces_axis, tiles),
        in_specs=[smem, smem] + [hbm] * 6,
        out_specs=[hbm, hbm, vmem],
        out_shape=[
            jax.ShapeDtypeStruct(field_in.shape, BF16),
            jax.ShapeDtypeStruct(field_in.shape, BF16),
            jax.ShapeDtypeStruct((2, 3 * C, 2 * LANES), F32),
        ],
        scratch_shapes=scratch,
        compiler_params=pltpu.CompilerParams(vmem_limit_bytes=57 << 20, collective_id=0, has_side_effects=True),
        cost_estimate=pl.CostEstimate(flops=flops, bytes_accessed=10**7, transcendentals=5 * 10**6),
    )(
        jnp.transpose(face_links, (2, 1, 0)), jnp.transpose(corner_rules), field_in, out_grad,
        taps_first(weight_first), taps_first(weight_second), bias_first[None], bias_second[None],
    )
    weight_shape = jax.ShapeDtypeStruct((3, 3, C, C), F32)
    bias_shape = jax.ShapeDtypeStruct((1, C), F32)
    face_spec = pl.BlockSpec((1, C, rows, width), lambda f: (f, 0, 0, 0))
    whole = lambda shape: pl.BlockSpec(shape, lambda f: (0,) * len(shape))
    output, grad_field, gw1, gb1, gw2, gb2 = pl.pallas_call(
        results_kernel,
        grid=(nf,),
        in_specs=[face_spec, face_spec, whole(sums.shape)],
        out_specs=[face_spec, face_spec] + [whole(a.shape) for a in (weight_shape, bias_shape) * 2],
        out_shape=[jax.ShapeDtypeStruct(field_in.shape, BF16)] * 2 + [weight_shape, bias_shape] * 2,
        compiler_params=pltpu.CompilerParams(vmem_limit_bytes=57 << 20),
    )(natural, last_rows, sums)
    back = lambda g: jnp.transpose(g, (2, 3, 0, 1))
    return output, grad_field, back(gw1), gb1[0], back(gw2), gb2[0]


def solution(mesh):
    cells = P("face", None, "tile", None)
    return jax.shard_map(
        body,
        mesh=mesh,
        in_specs=(cells, cells, P(), P(), P(), P(), P(), P()),
        out_specs=(cells, cells, P(), P(), P(), P()),
        check_vma=False,
    )
```

```python
import functools

import jax
import jax.numpy as jnp
from jax import lax
from jax.experimental import pallas as pl
from jax.experimental.pallas import tpu as pltpu
from jax.sharding import PartitionSpec as P

INV_ROOT_TWO = 0.7071067811865476
INV_ROOT_TWO_PI = 0.3989422804014327
F32 = jnp.float32
BF16 = jnp.bfloat16
LANES = 128
MESH_ID = pl.DeviceIdType.MESH
EDGES = 4
GROUP = 16


def gelu_pair(values):
    normal_cdf = 0.5 * (1.0 + lax.erf(values * INV_ROOT_TWO))
    normal_pdf = jnp.exp(-0.5 * values * values) * INV_ROOT_TWO_PI
    return (values * normal_cdf, normal_cdf + values * normal_pdf)


def one_hot(rows, target):
    row = lax.broadcasted_iota(jnp.int32, (rows, target.shape[1]), 0)
    return jnp.where(row == target, 1.0, 0.0).astype(BF16)


def turn(a, shift):
    return pltpu.roll(a, shift % LANES, 1)


def from_rows(src, dst, only=None):
    nf, rows, C, _ = src.shape
    for f in range(nf) if only is None else only:
        for r0 in range(0, rows, GROUP):
            n = min(GROUP, rows - r0)
            for c0 in range(0, C, GROUP):
                block = src[f, r0 : r0 + n, c0 : c0 + GROUP]
                if n < GROUP:
                    block = jnp.swapaxes(block.astype(F32), 0, 1).astype(BF16)
                else:
                    block = jnp.swapaxes(block, 0, 1)
                dst[f, c0 : c0 + GROUP, r0 : r0 + n] = block


def fused_kernel(
    faces_axis, tiles, links, rules, x_hbm, og_hbm, w1_hbm, w2_hbm, b1_hbm, b2_hbm,
    out_hbm, gf_hbm, gw_ref,
    x_ref, og_ref, w1_ref, w2_ref, b1_ref, b2_ref, s_in, s_out, pre_ref, we_place, ns_place,
    wst_ref, u_ref, b_ref,
    xb, hb, g2b, g1b, ogb, rowsb, slope_ref, cp, packs0, packs1, packs2, packs3, gp, gpn, full, seg_out, seg_in, line_in, ns_out, spread,
    addcol, addrow, part, landed,
    s_halo, r_halo, s_direct, s_fwd, s_ns, r_packs, s_ends, r_ends, s_seg, r_seg, s_sum, r_sum, s_res, r_res,
):
    nf, C, rows, width = x_ref.shape
    packs = (packs0, packs1, packs2, packs3)
    slots = packs0.shape[1]
    n_dev = faces_axis * tiles
    face = lax.axis_index("face")
    tile = lax.axis_index("tile")
    me = face * tiles + tile
    last = tiles - 1
    mirror_tile = last - tile
    half = tiles // 2
    lane = lax.broadcasted_iota(jnp.int32, (C, LANES), 1)
    even = lane % 2 == 0
    is_top = tile == 0
    is_bottom = tile == last
    top_f = jnp.where(is_top, 1.0, 0.0)
    bottom_f = jnp.where(is_bottom, 1.0, 0.0)
    upper_half = jnp.where(tile >= half, 1, 0)
    peer = lax.rem(face + 2, faces_axis)
    sibling = face + 1 - 2 * lax.rem(face, 2)
    sibling_peer = lax.rem(sibling + 2, faces_axis)

    def at(j):
        return (lax.div(j, tiles), lax.rem(j, tiles))

    def each_other(body):
        def step(j, carry):
            @pl.when(j != me)
            def _():
                body(j)

            return carry

        lax.fori_loop(0, n_dev, step, 0)

    barrier = pltpu.get_barrier_semaphore()
    each_other(lambda j: pl.semaphore_signal(barrier, inc=1, device_id=at(j), device_id_type=MESH_ID))

    inputs = [
        pltpu.make_async_copy(src, dst, s_in.at[i])
        for i, (src, dst) in enumerate(
            (
                (x_hbm, x_ref), (w1_hbm, w1_ref), (w2_hbm, w2_ref), (b1_hbm, b1_ref), (b2_hbm, b2_ref),
                (og_hbm, og_ref),
            )
        )
    ]
    for c in inputs:
        c.start()

    def to_rows(src, dst, first):
        for f in range(nf):
            for r0 in range(0, rows, GROUP):
                n = min(GROUP, rows - r0)
                for c0 in range(0, C, GROUP):
                    block = src[f, c0 : c0 + GROUP, r0 : r0 + n]
                    if n < GROUP:
                        block = jnp.swapaxes(block.astype(F32), 0, 1).astype(BF16)
                    else:
                        block = jnp.swapaxes(block, 0, 1)
                    dst[f, first + r0 : first + r0 + n, c0 : c0 + GROUP] = block

    def keep(acc, r, lo, hi):
        mixed = turn(jnp.where(lane == LANES - 1, hi, lo), 2 * r)
        return jnp.where((lane == 2 * r) | (lane == (2 * r - 1) % LANES), mixed, acc)

    def copy(src, dst, send, recv, device):
        return pltpu.make_async_remote_copy(src, dst, send, recv, device, MESH_ID)

    ns_base = 2 * faces_axis

    def halo_copies(k, buf):
        up = copy(buf.at[:, 1], buf.at[:, rows + 1], s_halo.at[k, 0], r_halo.at[k, 1], (face, tile - 1))
        down = copy(buf.at[:, rows], buf.at[:, 0], s_halo.at[k, 1], r_halo.at[k, 0], (face, tile + 1))
        return up, down

    def direct_copies(k):
        own = packs[k].at[face]
        here = face
        there = faces_axis + face
        return [
            copy(own, packs[k].at[there], s_direct.at[k, 0], r_packs.at[k, there], (face, mirror_tile)),
            copy(own, packs[k].at[there], s_direct.at[k, 1], r_packs.at[k, there], (peer, mirror_tile)),
            copy(own, packs[k].at[here], s_direct.at[k, 2], r_packs.at[k, here], (peer, tile)),
            copy(own, packs[k].at[here], s_direct.at[k, 3], r_packs.at[k, here], (sibling, tile)),
        ]

    def ns_slot():
        return ns_base + jnp.where(is_top, 0, 1) * faces_axis + face

    def ns_copies(k, j):
        t = jnp.where(is_top, last - j, j)
        src = ns_out.at[k, min(j, last - j)]
        slot = ns_slot()
        return [
            copy(src, packs[k].at[slot], s_ns.at[k, j], r_packs.at[k, slot], (face, t)),
            copy(src, packs[k].at[slot], s_ns.at[k, tiles + j], r_packs.at[k, slot], (peer, t)),
        ]

    def forward_slots():
        return [faces_axis + face, peer, faces_axis + peer] + [
            ns_base + n * faces_axis + q for n in range(2) for q in (face, peer)
        ]

    def arriving_slots():
        return [sibling, faces_axis + sibling, sibling_peer, faces_axis + sibling_peer] + [
            ns_base + n * faces_axis + q for n in range(2) for q in (sibling, sibling_peer)
        ]

    def forward_copy(k, i, slot):
        ref = packs[k].at[slot]
        return copy(ref, ref, s_fwd.at[k, i], r_packs.at[k, slot], (sibling, tile))

    def ends_copies(k):
        return (
            copy(gp.at[k], gpn.at[k, 1], s_ends.at[k, 0], r_ends.at[k, 1], (face, tile - 1)),
            copy(gp.at[k], gpn.at[k, 0], s_ends.at[k, 1], r_ends.at[k, 0], (face, tile + 1)),
        )

    def seg_copies(k):
        dst = seg_in.at[k, tile]
        return (
            copy(seg_out.at[k, 0], dst, s_seg.at[k, 0], r_seg.at[k, tile], (face, 0)),
            copy(seg_out.at[k, 1], dst, s_seg.at[k, 1], r_seg.at[k, tile], (face, last)),
        )

    def start_exchange(k, buf):
        for slot in range(slots):
            faces_here = [f for f in range(nf) if f // 2 == slot]
            packed = turn(cp[faces_here[0]], 1)
            if len(faces_here) > 1:
                packed = jnp.where(lane < 64, packed, turn(cp[faces_here[1]], 65))
            packs[k][face, slot] = packed.astype(BF16)
        for c in direct_copies(k):
            c.start()

        @pl.when(is_top | is_bottom)
        def _():
            lines = jnp.concatenate(
                [jnp.where(is_top, buf[f, 1].astype(F32), buf[f, rows].astype(F32)) for f in range(nf)], axis=0
            ).astype(BF16)
            spreads = jnp.dot(lines, spread[...], preferred_element_type=F32)
            for p in range(half):
                part_p = spreads[:, p * LANES : (p + 1) * LANES]
                for slot in range(slots):
                    faces_here = [f for f in range(nf) if f // 2 == slot]
                    first = faces_here[0]
                    packed = part_p[first * C : (first + 1) * C]
                    if len(faces_here) > 1:
                        packed = jnp.where(lane < 64, packed, turn(part_p[(first + 1) * C : (first + 2) * C], 64))
                    ns_out[k, p, slot] = packed.astype(BF16)
            packs[k][ns_slot()] = ns_out[k, 0]
            for j in range(tiles):
                same, across = ns_copies(k, j)
                across.start()
                if j < last:
                    same.start()

    def start_halo(k, buf):
        up, down = halo_copies(k, buf)

        @pl.when(jnp.logical_not(is_top))
        def _():
            up.start()

        @pl.when(jnp.logical_not(is_bottom))
        def _():
            down.start()

    def not_own_ns(i):
        n, which = divmod(i - 3, 2)
        if which:
            return jnp.bool_(True)
        return jnp.logical_not(is_top if n == 0 else is_bottom)

    def forward_exchange(k):
        for i, slot in enumerate(forward_slots()):
            fwd = forward_copy(k, i, slot)
            if i < 3:
                fwd.wait_recv()
            else:

                @pl.when(not_own_ns(i))
                def _():
                    fwd.wait_recv()

            fwd.start()

    def link(f, e):
        return links[0, e, face * nf + f], links[1, e, face * nf + f], links[2, e, face * nf + f]

    def source(f, e):
        g, e2, flip = link(f, e)
        q2, f2 = lax.div(g, nf), lax.rem(g, nf)
        we = lax.div(e2, 2)
        idx = we * (flip * faces_axis + q2) + (1 - we) * (ns_base + e2 * faces_axis + q2)
        return idx, lax.div(f2, 2)

    def source_lanes(f, e):
        g, e2, flip = link(f, e)
        we = lax.div(e2, 2)
        other = upper_half + flip - 2 * upper_half * flip
        bit = we * (3 - e2) + (1 - we) * (1 - other)
        return 64 * lax.rem(lax.rem(g, nf), 2) + bit + flip * 2 * (rows - 1), 2 - 4 * flip

    def place_sources():
        d = lax.broadcasted_iota(jnp.int32, (1, LANES), 1)
        west_r = d // 2
        west_ok = (d % 2 == 0) & (d < 2 * rows)
        east_r = ((d + 1) % LANES) // 2
        east_ok = (d % 2 == 1) & (east_r < rows)
        for f in range(nf):
            for j, (e, ok, r) in enumerate(((2, west_ok, west_r), (3, east_ok, east_r))):
                start, step = source_lanes(f, e)
                we_place[f, j * LANES : (j + 1) * LANES] = one_hot(LANES, jnp.where(ok, start + step * r, -1))
            ok = (d >= f * rows) & (d < (f + 1) * rows)
            for e in range(2):
                start, step = source_lanes(f, e)
                ns_place[e, f * LANES : (f + 1) * LANES] = one_hot(
                    LANES, jnp.where(ok, start + step * (d - f * rows), -1)
                )

    def pick(k):
        for slot in arriving_slots():
            copy(packs[k].at[slot], packs[k].at[slot], s_fwd.at[k, 0], r_packs.at[k, slot], (sibling, tile)).wait_recv()

        def taken(f, e):
            idx, slot = source(f, e)
            return packs[k][idx, slot]

        for e in range(2):
            srcs = jnp.concatenate([taken(f, e) for f in range(nf)], axis=1)
            seg_out[k, e] = jnp.dot(srcs, ns_place[e], preferred_element_type=F32).astype(BF16)
        for f in range(nf):
            srcs = jnp.concatenate([taken(f, 2), taken(f, 3)], axis=1)
            gp[k, f] = jnp.dot(srcs, we_place[f], preferred_element_type=F32).astype(BF16)
        up, down = ends_copies(k)
        to_top, to_bottom = seg_copies(k)

        @pl.when(is_top)
        def _():
            seg_in[k, 0] = seg_out[k, 0]

        @pl.when(is_bottom)
        def _():
            seg_in[k, last] = seg_out[k, 1]

        @pl.when(jnp.logical_not(is_top))
        def _():
            to_top.start()
            up.start()

        @pl.when(jnp.logical_not(is_bottom))
        def _():
            to_bottom.start()
            down.start()

        for f in range(nf):
            full[k, f] = gp[k, f].astype(F32)

    def stack3(a, first):
        return [turn(a, first), a, turn(a, -first)]

    def columns_forward(k, which):
        w = wst_ref[which]
        for f in range(nf):
            stacked = jnp.concatenate(stack3(full[k, f], 2), axis=0).astype(BF16)
            y = jnp.dot(w, stacked, preferred_element_type=F32)
            addcol[f] = jnp.where(even, y[:C], y[2 * C :])

    def end_rules(f, e):
        g, e2, flip = link(f, e)
        we = lax.div(e2, 2)
        first = rules[we * (e2 - 2) + (1 - we) * 2 * e2, g]
        final = rules[we * e2 + (1 - we) * (1 + 2 * e2), g]
        first = jnp.where(first == we, 1.0, 0.0)
        final = jnp.where(final == we, 1.0, 0.0)
        low = jnp.where(flip == 0, first, final)
        high = jnp.where(flip == 0, final, first)
        return e2 * 2 + flip, low, high

    def columns_backward(k, which):
        for f in range(nf):
            wu, wlow, whigh = end_rules(f, 2)
            eu, elow, ehigh = end_rules(f, 3)
            a = full[k, f]
            low = jnp.where(lane == 0, wlow, jnp.where(lane == LANES - 1, elow, 0.0)) * top_f
            high = jnp.where(lane == 2 * rows - 2, whigh, jnp.where(lane == 2 * rows - 3, ehigh, 0.0)) * bottom_f
            stacked = jnp.concatenate(stack3(a, -2) + [a * low, a * high], axis=0).astype(BF16)
            weights = jnp.concatenate([u_ref[which, wu], u_ref[which, eu]], axis=0)
            y = jnp.dot(weights, stacked, preferred_element_type=F32)
            addcol[f] = jnp.where(even, y[:C], y[C:]).astype(BF16).astype(F32)

    def finish_ends(k, buf, which, forward):
        above = (lane == LANES - 2) | (lane == LANES - 3)
        below = (lane == 2 * rows) | (lane == 2 * rows - 1)

        @pl.when(jnp.logical_not(is_top))
        def _():
            copy(gpn.at[k, 0], gpn.at[k, 0], s_ends.at[k, 0], r_ends.at[k, 0], (face, tile - 1)).wait_recv()
            copy(buf.at[:, 0], buf.at[:, 0], s_halo.at[k, 0], r_halo.at[k, 0], (face, tile - 1)).wait_recv()
            for f in range(nf):
                full[k, f] = jnp.where(above, turn(gpn[k, 0, f].astype(F32), -2 * rows), full[k, f])

        @pl.when(jnp.logical_not(is_bottom))
        def _():
            copy(gpn.at[k, 1], gpn.at[k, 1], s_ends.at[k, 1], r_ends.at[k, 1], (face, tile + 1)).wait_recv()
            hup_ref = buf.at[:, rows + 1]
            copy(hup_ref, hup_ref, s_halo.at[k, 1], r_halo.at[k, 1], (face, tile + 1)).wait_recv()
            for f in range(nf):
                full[k, f] = jnp.where(below, turn(gpn[k, 1, f].astype(F32), 2 * rows), full[k, f])

        def assemble(e):
            for t in range(tiles):

                @pl.when(tile != t)
                def _():
                    ref = seg_in.at[k, t]
                    copy(ref, ref, s_seg.at[k, 0], r_seg.at[k, t], (face, last - tile)).wait_recv()

            for f in range(nf):
                for i in range(width // LANES):
                    piece = jnp.zeros((C, LANES), F32)
                    for t in range(tiles):
                        if t * rows // LANES == i:
                            off = t * rows % LANES
                            moved = turn(seg_in[k, t].astype(F32), off - f * rows)
                            piece = jnp.where((lane >= off) & (lane < off + rows), moved, piece)
                    line_in[f, :, i * LANES : (i + 1) * LANES] = piece

            if forward:
                row = 0 if e == 0 else rows + 1
                for f in range(nf):
                    line = line_in[f]
                    buf[f, row] = line.astype(BF16)
                    ghost = full[k, f]
                    mixed = jnp.where(lane == LANES - 1, line[:, -LANES:], line[:, :LANES])
                    by_line_w = rules[2 * e, face * nf + f] == 0
                    by_line_e = rules[2 * e + 1, face * nf + f] == 0
                    if e == 0:
                        from_line, from_col = turn(mixed, -2), turn(ghost, -2)
                        at_w, at_e = LANES - 2, LANES - 3
                    else:
                        from_line, from_col = turn(mixed, 2 * rows), turn(ghost, 2)
                        at_w, at_e = 2 * rows, 2 * rows - 1
                    corner_w = jnp.where(by_line_w, from_line, from_col)
                    corner_e = jnp.where(by_line_e, from_line, from_col)
                    full[k, f] = jnp.where(lane == at_w, corner_w, jnp.where(lane == at_e, corner_e, ghost))
            else:
                row = 0 if e == 0 else rows + 1
                wide = lax.broadcasted_iota(jnp.int32, (C, width), 1)
                for f in range(nf):
                    buf[f, row] = jnp.zeros((C, width), BF16)
                    u, low, high = end_rules(f, e)
                    line = line_in[f]
                    ahead = jnp.where(wide == width - 1, 0.0, pltpu.roll(line, width - 1, 1))
                    behind = jnp.where(wide == 0, 0.0, pltpu.roll(line, 1, 1))
                    ends = [
                        line * jnp.where(wide == 0, low, 0.0), line * jnp.where(wide == width - 1, high, 0.0)
                    ]
                    stacked = jnp.concatenate([ahead, line, behind] + ends, axis=0).astype(BF16)
                    y = jnp.dot(u_ref[which, u], stacked, preferred_element_type=F32)
                    addrow[e, f] = y.astype(BF16).astype(F32)

        @pl.when(is_top)
        def _():
            assemble(0)

        @pl.when(is_bottom)
        def _():
            assemble(1)

    def cut(a, i):
        return a[:, i * LANES : (i + 1) * LANES]

    def conv_row(w, buf, f, r, ins):
        y = jnp.dot(w, buf[f, pl.ds(r, 3)].reshape(3 * C, width), preferred_element_type=F32)
        first, final = lane == 0, lane == LANES - 1
        parts = width // LANES
        west = [turn(cut(y[:C], i), 1) for i in range(parts)]
        east = [turn(cut(y[2 * C :], i), -1) for i in range(parts)]
        out = []
        for i in range(parts):
            left = jnp.where(first, west[i - 1] if i > 0 else ins, west[i])
            right = jnp.where(final, east[i + 1] if i < parts - 1 else ins, east[i])
            out.append(cut(y[C : 2 * C], i) + left + right)
        return out

    def run_inner_products(which, buf):
        def face_step(f, carry):
            w = wst_ref[which]
            zero = jnp.zeros((C, LANES), F32)
            for r in range(1, rows - 1):
                for i, p in enumerate(conv_row(w, buf, f, r, zero)):
                    pre_ref[f, r, :, i * LANES : (i + 1) * LANES] = p
            return carry

        lax.fori_loop(0, nf, face_step, 0)

    def with_columns(f, r, ghost):
        ins = turn(ghost, -2 * r)
        total = [cut(pre_ref[f, r], i) for i in range(width // LANES)]
        total[0] = total[0] + jnp.where(lane == 0, ins, 0.0)
        total[-1] = total[-1] + jnp.where(lane == LANES - 1, ins, 0.0)
        return total

    def do_rows(which, buf, f, rs, finish, acc):
        ghost = addcol[f]
        for r in rs:
            if r in (0, rows - 1):
                total = conv_row(wst_ref[which], buf, f, r, turn(ghost, -2 * r))
            else:
                total = with_columns(f, r, ghost)
            kept = finish(f, r, total)
            if kept is not None:
                acc = keep(acc, r, kept[0], kept[-1])
        return acc

    def run_inner(which, buf, finish):
        def face_step(f, carry):
            cp[f] = do_rows(which, buf, f, range(1, rows - 1), finish, jnp.zeros((C, LANES), F32))
            return carry

        lax.fori_loop(0, nf, face_step, 0)

    def run_outer(which, buf, finish):
        accs = [do_rows(which, buf, f, (0, rows - 1), finish, cp[f]) for f in range(nf)]
        for f in range(nf):
            cp[f] = accs[f]

    def put(ref, f, r, parts, dtype):
        ref[f, r] = jnp.concatenate([p.astype(dtype) for p in parts], axis=1)

    def bias(i):
        return jnp.broadcast_to(b_ref[i], (C, LANES))

    def finish_first(f, r, total):
        pairs = [gelu_pair(p + bias(0)) for p in total]
        values = [p[0] for p in pairs]
        put(slope_ref, f, r, [p[1] for p in pairs], F32)
        put(hb, f, r + 1, values, BF16)
        return values

    def finish_second(f, r, total):
        pairs = [gelu_pair(p + bias(1)) for p in total]
        put(rowsb, f, r, [p[0] for p in pairs], BF16)
        og = ogb[f, r].astype(F32)
        grads = [og[:, i * LANES : (i + 1) * LANES] * p[1] for i, p in enumerate(pairs)]
        put(g2b, f, r + 1, grads, BF16)
        return grads

    def with_row(f, r, total):
        if r not in (0, rows - 1):
            return total
        e = 0 if r == 0 else 1
        return [p + addrow[e, f, :, i * LANES : (i + 1) * LANES] for i, p in enumerate(total)]

    def finish_third(f, r, total):
        total = with_row(f, r, total)
        slope = slope_ref[f, r]
        grads = [p * slope[:, i * LANES : (i + 1) * LANES] for i, p in enumerate(total)]
        put(g1b, f, r + 1, grads, BF16)
        return grads

    def finish_last(f, r, total):
        put(rowsb, f, r, with_row(f, r, total), BF16)
        return None

    def weight_products(i, grad_buf, field_buf, k):
        part[i] = jnp.zeros_like(part[i])
        ones = jnp.ones((16, width), BF16)

        def face_step(f, carry):
            first, final = lane == 0, lane == LANES - 1
            zero = jnp.zeros((C, LANES), F32)
            lefts, rights = [], []
            for r in range(rows):
                grad = grad_buf[f, r + 1]
                wide = grad.astype(F32)
                cuts = [wide[:, j : j + LANES] for j in range(0, width, LANES)]
                ahead = [turn(a, -1) for a in cuts]
                behind = [turn(a, 1) for a in cuts]
                n = len(cuts)
                shift_a = [jnp.where(final, ahead[j + 1] if j < n - 1 else zero, ahead[j]) for j in range(n)]
                shift_b = [jnp.where(first, behind[j - 1] if j > 0 else zero, behind[j]) for j in range(n)]
                lefts.append(
                    jnp.concatenate(
                        [
                            jnp.concatenate([a.astype(BF16) for a in shift_a], axis=1),
                            grad,
                            jnp.concatenate([b.astype(BF16) for b in shift_b], axis=1),
                        ],
                        axis=0,
                    )
                )
                rights.append(
                    jnp.concatenate([field_buf[f, pl.ds(r, 3)].reshape(3 * C, width), ones], axis=0)
                )
            inside = (lane < 2 * rows - 1) | (lane == LANES - 1)
            edge = jnp.where(inside, cp[f], 0.0)
            lefts.append(
                jnp.concatenate([jnp.where(even, edge, 0.0), zero, jnp.where(even, 0.0, edge)], axis=0).astype(BF16)
            )
            rights.append(
                jnp.concatenate(stack3(full[k, f], 2) + [jnp.zeros((16, LANES), F32)], axis=0).astype(BF16)
            )
            products = lax.dot_general(
                jnp.concatenate(lefts, axis=1),
                jnp.concatenate(rights, axis=1),
                (((1,), (1,)), ((), ())),
                preferred_element_type=F32,
            )
            part[i, :, : 3 * C + 16] += products
            return carry

        lax.fori_loop(0, nf, face_step, 0)

    block = 8
    per = 3 * C // block
    middle = max(tiles - 2, 1)

    def owner(i, o):
        j = o + 6 * i
        return (j // middle % faces_axis, 1 + j % middle)

    def is_owner(i, o):
        f, t = owner(i, o)
        return (face == f) & (tile == t)

    def block_of(ref, i, o):
        return ref.at[i, pl.ds(o * block, block)]

    def sum_copy(i, o):
        return copy(block_of(part, i, o), landed.at[i, me], s_sum.at[i, o], r_sum.at[i, me], owner(i, o))

    def start_sums(i):
        for o in range(per):
            c = sum_copy(i, o)

            @pl.when(jnp.logical_not(is_owner(i, o)))
            def _():
                c.start()

    def result_copy(i, o, j):
        ref = block_of(gw_ref, i, o)
        return copy(ref, ref, s_res.at[i, j], r_res.at[i, o], at(j))

    def add_sums(i):
        for o in range(per):

            @pl.when(is_owner(i, o))
            def _():
                each_other(
                    lambda j: copy(
                        landed.at[i, j], landed.at[i, j], s_sum.at[i, 0], r_sum.at[i, j], at(j)
                    ).wait_recv()
                )
                landed[i, me] = block_of(part, i, o)[...]
                total = lax.fori_loop(1, n_dev, lambda j, t: t + landed[i, j], landed[i, 0])
                block_of(gw_ref, i, o)[...] = total
                each_other(lambda j: result_copy(i, o, j).start())

    def place_weights():
        def blocks(count, places):
            row = lax.broadcasted_iota(jnp.int32, (C, count * C), 0)
            column = lax.broadcasted_iota(jnp.int32, (C, count * C), 1)
            hit = functools.reduce(jnp.logical_or, [column == row + p * C for p in places])
            return jnp.where(hit, 1.0, 0.0).astype(BF16)

        thirds = [blocks(3, [k]) for k in range(3)]
        straight = lambda a, e: jnp.dot(a, e, preferred_element_type=F32)
        turned = lambda a, e: lax.dot_general(a, e, (((0,), (0,)), ((), ())), preferred_element_type=F32)
        for which, w in ((0, w1_ref), (1, w2_ref)):
            for l in range(3):
                total = sum(straight(w[k, l], thirds[k]) for k in range(3))
                wst_ref[which, l * C : (l + 1) * C] = total.astype(BF16)
        for which, w in ((2, w2_ref), (3, w1_ref)):
            for l in range(3):
                total = sum(turned(w[2 - k, 2 - l], thirds[k]) for k in range(3))
                wst_ref[which, l * C : (l + 1) * C] = total.astype(BF16)
        row = lax.broadcasted_iota(jnp.int32, (C, C), 0)
        column = lax.broadcasted_iota(jnp.int32, (C, C), 1)
        for i, b in enumerate((b1_ref, b2_ref)):
            b_ref[i] = jnp.broadcast_to(
                jnp.sum(jnp.where(row == column, jnp.broadcast_to(b[...], (C, C)), 0.0), axis=1, keepdims=True),
                (C, LANES),
            )

    def place_taps():
        def blocks(places):
            row = lax.broadcasted_iota(jnp.int32, (C, 5 * C), 0)
            column = lax.broadcasted_iota(jnp.int32, (C, 5 * C), 1)
            hit = functools.reduce(jnp.logical_or, [column == row + p * C for p in places])
            return jnp.where(hit, 1.0, 0.0).astype(BF16)

        fifths = [blocks([0, 3]), blocks([1]), blocks([2, 4])]
        for i, w in enumerate((w2_ref, w1_ref)):
            for e in range(EDGES):
                for flip in range(2):
                    total = jnp.zeros((C, 5 * C), F32)
                    for m in range(3):
                        n = 2 - m if flip else m
                        tap = (w[0, n], w[2, n], w[n, 0], w[n, 2])[e]
                        total += lax.dot_general(
                            tap, fifths[m], (((0,), (0,)), ((), ())), preferred_element_type=F32
                        )
                    u_ref[i, 2 * e + flip] = total.astype(BF16)

    inputs[0].wait()
    to_rows(x_ref, xb, 1)

    def first_columns(f, carry):
        acc = jnp.zeros((C, LANES), F32)
        for r in range(rows):
            row = xb[f, r + 1].astype(F32)
            acc = keep(acc, r, row[:, :LANES], row[:, -LANES:])
        cp[f] = acc
        return carry

    lax.fori_loop(0, nf, first_columns, 0)
    d = lax.broadcasted_iota(jnp.int32, (1, LANES), 1)
    for p in range(half):
        seg = jnp.where(d % 2 == 1, p, last - p)
        target = jnp.where(d < 2 * rows, seg * rows + d // 2, -1)
        spread[:, p * LANES : (p + 1) * LANES] = one_hot(width, target)
    addrow[...] = jnp.zeros_like(addrow)
    pl.semaphore_wait(barrier, n_dev - 1)

    start_exchange(0, xb)
    for c in inputs[1:]:
        c.wait()
    place_weights()
    run_inner_products(0, xb)
    forward_exchange(0)
    start_halo(0, xb)
    place_sources()
    to_rows(og_ref, ogb, 0)
    pick(0)
    columns_forward(0, 0)
    run_inner(0, xb, finish_first)
    finish_ends(0, xb, None, True)
    columns_forward(0, 0)
    run_outer(0, xb, finish_first)

    start_exchange(1, hb)
    place_taps()
    run_inner_products(1, hb)
    forward_exchange(1)
    start_halo(1, hb)
    pick(1)
    columns_forward(1, 1)
    run_inner(1, hb, finish_second)
    finish_ends(1, hb, None, True)
    columns_forward(1, 1)
    run_outer(1, hb, finish_second)

    start_exchange(2, g2b)
    weight_products(0, g2b, hb, 1)
    from_rows(rowsb, x_ref)
    out_copy = pltpu.make_async_copy(x_ref, out_hbm, s_out.at[nf])
    out_copy.start()
    run_inner_products(2, g2b)
    forward_exchange(2)
    start_halo(2, g2b)
    pick(2)
    start_sums(0)
    columns_backward(2, 0)
    run_inner(2, g2b, finish_third)
    finish_ends(2, g2b, 0, False)
    columns_backward(2, 0)
    run_outer(2, g2b, finish_third)

    start_exchange(3, g1b)
    weight_products(1, g1b, xb, 0)
    start_sums(1)
    add_sums(0)
    run_inner_products(3, g1b)
    forward_exchange(3)
    start_halo(3, g1b)
    pick(3)
    columns_backward(3, 1)
    add_sums(1)
    run_inner(3, g1b, finish_last)
    finish_ends(3, g1b, 1, False)
    columns_backward(3, 1)
    run_outer(3, g1b, finish_last)

    gf_copies = [pltpu.make_async_copy(og_ref.at[f], gf_hbm.at[f], s_out.at[f]) for f in range(nf)]
    for f in range(nf):
        from_rows(rowsb, og_ref, [f])
        gf_copies[f].start()

    for i in range(2):
        for o in range(per):

            @pl.when(jnp.logical_not(is_owner(i, o)))
            def _():
                result_copy(i, o, me).wait_recv()
                sum_copy(i, o).wait_send()

            @pl.when(is_owner(i, o))
            def _():
                each_other(lambda j: result_copy(i, o, j).wait_send())

    out_copy.wait()
    for c in gf_copies:
        c.wait()
    for k, buf in enumerate((xb, hb, g2b, g1b)):
        for c in direct_copies(k):
            c.wait_send()
        for i, slot in enumerate(forward_slots()):
            forward_copy(k, i, slot).wait_send()
        ups = (halo_copies(k, buf)[0], ends_copies(k)[0], seg_copies(k)[0])
        downs = (halo_copies(k, buf)[1], ends_copies(k)[1], seg_copies(k)[1])

        @pl.when(jnp.logical_not(is_top))
        def _():
            for c in ups:
                c.wait_send()

        @pl.when(jnp.logical_not(is_bottom))
        def _():
            for c in downs:
                c.wait_send()

        @pl.when(is_top | is_bottom)
        def _():
            for j in range(tiles):
                same, across = ns_copies(k, j)
                across.wait_send()
                if j < last:
                    same.wait_send()


def results_kernel(out_ref, last_ref, sums_ref, out_dst, gf_dst, gw1, gb1, gw2, gb2):
    C = gw1.shape[-1]
    width = out_ref.shape[-1]
    out_dst[...] = out_ref[...]
    gf_dst[...] = last_ref[...]

    @pl.when(pl.program_id(0) == 0)
    def _():
        row = lax.broadcasted_iota(jnp.int32, (C, C), 0)
        column = lax.broadcasted_iota(jnp.int32, (C, C), 1)
        for i, (gw, gb) in enumerate(((gw2, gb2), (gw1, gb1))):
            for l in range(3):
                wide = sums_ref[i, l * C : (l + 1) * C] * (1.0 / width)
                for k in range(3):
                    gw[k, l] = pltpu.roll(wide, -k * C % (2 * LANES), 1)[:, :C]
                if l == 1:
                    at_first = pltpu.roll(wide, -3 * C % (2 * LANES), 1)[:, :1]
                    spread = jnp.where(row == column, jnp.broadcast_to(at_first, (C, C)), 0.0)
                    gb[...] = jnp.sum(spread, axis=0, keepdims=True)


def body(field_in, out_grad, weight_first, bias_first, weight_second, bias_second, face_links, corner_rules):
    faces_axis, tiles = lax.axis_size("face"), lax.axis_size("tile")
    nf, C, rows, width = field_in.shape
    n_dev = faces_axis * tiles
    taps_first = lambda w: jnp.transpose(w, (2, 3, 0, 1))
    slots = (nf + 1) // 2
    vm = pltpu.VMEM
    dma = pltpu.SemaphoreType.DMA
    padded = vm((nf, rows + 2, C, width), BF16)
    per = 3 * C // 8
    scratch = [
        vm(field_in.shape, BF16), vm(field_in.shape, BF16),
        vm((3, 3, C, C), BF16), vm((3, 3, C, C), BF16), vm((1, C), F32), vm((1, C), F32), dma((6,)), dma((nf + 1,)),
        vm((nf, rows, C, width), F32),
        vm((nf, 2 * LANES, LANES), BF16), vm((2, nf * LANES, LANES), BF16),
        vm((4, 3 * C, 3 * C), BF16),
        vm((2, 2 * EDGES, C, 5 * C), BF16),
        vm((2, C, LANES), F32),
        padded, padded, padded, padded,
        vm((nf, rows, C, width), BF16),
        vm((nf, rows, C, width), BF16),
        vm((nf, rows, C, width), F32),
        vm((nf, C, LANES), F32),
        *[vm((4 * faces_axis, slots, C, LANES), BF16)] * 4,
        vm((4, nf, C, LANES), BF16),
        vm((4, 2, nf, C, LANES), BF16),
        vm((4, nf, C, LANES), F32),
        vm((4, 2, C, LANES), BF16),
        vm((4, tiles, C, LANES), BF16),
        vm((nf, C, width), F32),
        vm((4, tiles // 2, slots, C, LANES), BF16),
        vm((width, tiles // 2 * LANES), BF16),
        vm((nf, C, LANES), F32),
        vm((2, nf, C, width), F32),
        vm((2, 3 * C, 2 * LANES), F32),
        vm((2, n_dev, 8, 2 * LANES), F32),
        dma((4, 2)), dma((4, 2)), dma((4, 4)), dma((4, 7)), dma((4, 2 * tiles)), dma((4, 4 * faces_axis)),
        dma((4, 2)), dma((4, 2)), dma((4, 2)), dma((4, tiles)),
        dma((2, per)), dma((2, n_dev)), dma((2, n_dev)), dma((2, per)),
    ]
    vmem = pl.BlockSpec(memory_space=pltpu.VMEM)
    smem = pl.BlockSpec(memory_space=pltpu.SMEM)
    hbm = pl.BlockSpec(memory_space=pltpu.HBM)
    flops = 2 * 6 * 9 * C * C * nf * rows * width
    natural, last_rows, sums = pl.pallas_call(
        functools.partial(fused_kernel, faces_axis, tiles),
        in_specs=[smem, smem] + [hbm] * 6,
        out_specs=[hbm, hbm, vmem],
        out_shape=[
            jax.ShapeDtypeStruct(field_in.shape, BF16),
            jax.ShapeDtypeStruct(field_in.shape, BF16),
            jax.ShapeDtypeStruct((2, 3 * C, 2 * LANES), F32),
        ],
        scratch_shapes=scratch,
        compiler_params=pltpu.CompilerParams(vmem_limit_bytes=57 << 20, collective_id=0, has_side_effects=True),
        cost_estimate=pl.CostEstimate(flops=flops, bytes_accessed=10**7, transcendentals=5 * 10**6),
    )(
        jnp.transpose(face_links, (2, 1, 0)), jnp.transpose(corner_rules), field_in, out_grad,
        taps_first(weight_first), taps_first(weight_second), bias_first[None], bias_second[None],
    )
    weight_shape = jax.ShapeDtypeStruct((3, 3, C, C), F32)
    bias_shape = jax.ShapeDtypeStruct((1, C), F32)
    face_spec = pl.BlockSpec((1, C, rows, width), lambda f: (f, 0, 0, 0))
    whole = lambda shape: pl.BlockSpec(shape, lambda f: (0,) * len(shape))
    output, grad_field, gw1, gb1, gw2, gb2 = pl.pallas_call(
        results_kernel,
        grid=(nf,),
        in_specs=[face_spec, face_spec, whole(sums.shape)],
        out_specs=[face_spec, face_spec] + [whole(a.shape) for a in (weight_shape, bias_shape) * 2],
        out_shape=[jax.ShapeDtypeStruct(field_in.shape, BF16)] * 2 + [weight_shape, bias_shape] * 2,
        compiler_params=pltpu.CompilerParams(vmem_limit_bytes=57 << 20),
    )(natural, last_rows, sums)
    back = lambda g: jnp.transpose(g, (2, 3, 0, 1))
    return output, grad_field, back(gw1), gb1[0], back(gw2), gb2[0]


def solution(mesh):
    cells = P("face", None, "tile", None)
    return jax.shard_map(
        body,
        mesh=mesh,
        in_specs=(cells, cells, P(), P(), P(), P(), P(), P()),
        out_specs=(cells, cells, P(), P(), P(), P()),
        check_vma=False,
    )
```
